32 devices in a mesh: groups: 2 (over x), tok: 16 (over z, y, core).
Axes of the slice: x: 2, y: 2, z: 4, core: 2. Of those that a mesh axis runs over, the one named last changes fastest.
Arguments:
- queries: bfloat16 [16384, 2048], P(('groups', 'tok')), parts along dimension 0, may hold values from -6 to 6
- keys: bfloat16 [16384, 2048], P(('groups', 'tok')), parts along dimension 0, may hold values from -6 to 6
- values: bfloat16 [16384, 2048], P(('groups', 'tok')), parts along dimension 0, may hold values from -6 to 6
- rates: float32 [16384, 4], P(('groups', 'tok')), parts along dimension 0, may hold values from 0.00024414062 to 0.001953125
- split_row: int32 [32], P(('groups', 'tok')), parts along dimension 0, may hold values from 128 to 384, as said below
- fast_init: float32 [512, 3072], P('tok'), may hold values from -0.25 to 0.25
Outputs:
- mixed: bfloat16 [16384, 2048], P(('groups', 'tok')), parts along dimension 0
The draws below stay inside these ranges and needn't reach their ends.
There are 2 independent parts, one for each index of `groups`. The reference program is written for one: setup_inputs(seed, part) draws one part's arguments, and reference() takes and returns one part's arrays. A program takes and returns all parts, laid end to end along the dimension named above; an argument that names none is the same for every part. Nothing has to cross between parts.
Inputs may be any that keep to these rules, and one draw needn't show every extreme that they name: `split_row`: some index of tok has exactly 128 and some exactly 384.
All inputs are finite; a program needn't handle non-finite values.
Results may differ from the reference program's by a relative error of at most 0.012.
The reference program's roundings to bfloat16 on the way count: a program that leaves them out, or rounds other values in their place, can miss the bound.
Values may be sent and summed in bfloat16 or wider, within the bound.
A program may use at most 128 MiB of HBM per device.

```python
import math
import jax
import jax.numpy as jnp
from jax import lax

HEADS = 4
DK = 512
FH = 256
TOK_DEV = 512
TOKENS = 8192
N_TOK = 16


def draw_split_row(key, part):
    lowest = TOK_DEV // 4
    highest = 3 * TOK_DEV // 4
    first_key, second_key, third_key = jax.random.split(key, 3)
    picked = jax.random.randint(first_key, (N_TOK,), lowest, highest + 1)
    low_place = jax.random.randint(second_key, (), 0, N_TOK)
    high_place = (low_place + jax.random.randint(third_key, (), 1, N_TOK)) % N_TOK
    picked = picked.at[low_place].set(lowest).at[high_place].set(highest)
    return picked.astype(jnp.int32)


def with_spikes(array, key, source, target, blocks, factor):
    owner, partner = [(jnp.arange(array.shape[position]) // (array.shape[position] // blocks)).reshape([-1 if axis == position else 1 for axis in range(array.ndim)]) for position in (source, target)]
    chosen = jax.random.permutation(key, blocks)[partner]
    strong = (owner == chosen) | (owner == (partner + blocks // 2) % blocks)
    return jnp.where(strong, factor * array, array)


def block_scale(stream_key, extent, cuts, low, high):
    def one(dim, blocks):
        draws = jax.random.uniform(jax.random.fold_in(jax.random.fold_in(stream_key, 6), dim), (blocks,), jnp.float32, low / len(cuts), high / len(cuts))
        return jnp.repeat(jnp.exp(draws), extent[dim] // blocks).reshape((-1,) + (1,) * (len(extent) - dim - 1))

    loudness = one(*cuts[0])
    for cut in cuts[1:]:
        loudness = loudness * one(*cut)
    return loudness


def noise(own_key, shape, width, reach, cuts=(), dtype=jnp.bfloat16):
    drawn = width * jax.random.normal(own_key, shape, jnp.float32)
    if cuts:
        drawn = drawn * block_scale(own_key, shape, cuts, -0.22, 0.18)
    return jnp.clip(drawn, -reach, reach).astype(dtype)


def gaussian_with(rng, dims, spread, bound, shards, heavy, dtype=jnp.bfloat16):
    array = spread * jax.random.normal(rng, dims, jnp.float32)
    if shards:
        array = array * block_scale(rng, dims, shards, -0.22, 0.18)
    return jnp.clip(with_spikes(array, jax.random.fold_in(rng, 3), *heavy), -bound, bound).astype(dtype)


def setup_inputs(seed: int = 0, part: int = 0) -> dict:
    key_of = jax.random.split(jax.random.key(seed), 7)
    own_keys = jax.random.split(jax.random.fold_in(key_of[6], part), 7)
    return {
        "queries": noise(own_keys[0], (TOKENS, HEADS * DK), 1.0, 6.0, ((0, 16),)),
        "keys": gaussian_with(own_keys[1], (TOKENS, HEADS * DK), 1.0, 6.0, ((0, 16),), (0, 1, 16, 2.0)),
        "values": gaussian_with(own_keys[2], (TOKENS, HEADS * DK), 1.0, 6.0, ((0, 16),), (0, 1, 16, 2.0)),
        "rates": jnp.clip(jnp.exp(math.log(0.001953125) - 2.0794415 * jax.random.uniform(own_keys[3], (TOKENS, HEADS), jnp.float32) ** block_scale(own_keys[3], (TOKENS, HEADS), ((0, 16),), -0.2, 0.2)), 0.00024414062, 0.001953125),
        "split_row": draw_split_row(jax.random.fold_in(jax.random.fold_in(key_of[6], part), 71), part),
        "fast_init": noise(key_of[5], (DK, 3 * HEADS * FH), DK ** -0.5, 0.25, ((0, 16),), jnp.float32),
    }


def forward_heads(inputs, weights):
    gates = jnp.einsum('rhj,jhf->rhf', inputs, weights[:, 0])
    ups = jnp.einsum('rhj,jhf->rhf', inputs, weights[:, 1])
    return (gates, ups)

def normalize_rows(moved, initial):
    target = jnp.sqrt(lax.optimization_barrier(jnp.mean(initial * initial, axis=-1, keepdims=True)))
    current = jnp.sqrt(lax.optimization_barrier(jnp.mean(moved * moved, axis=-1, keepdims=True)) + 1e-06)
    return moved * (target / current)

def reference(queries, keys, values, rates, split_row, fast_init):
    query_heads = queries.astype(jnp.float32).reshape(TOKENS, HEADS, DK)
    key_heads = keys.astype(jnp.float32).reshape(TOKENS, HEADS, DK)
    value_heads = values.astype(jnp.float32).reshape(TOKENS, HEADS, DK)
    positions = jnp.arange(TOKENS)
    local_rows = positions % TOK_DEV
    owners = positions // TOK_DEV
    first = local_rows < split_row[owners]
    initial = fast_init.reshape(DK, 3, HEADS, FH)
    state = initial
    momentum = jnp.zeros_like(initial)
    results = []
    for segment in range(2):
        keep = first if segment == 0 else jnp.logical_not(first)
        weights = state.astype(jnp.bfloat16).astype(jnp.float32)
        gates, ups = forward_heads(key_heads, weights)
        sigma = jax.nn.sigmoid(gates)
        active = gates * sigma
        hidden_act = (active * ups).astype(jnp.bfloat16).astype(jnp.float32)
        scale = -(rates * keep[:, None].astype(jnp.float32))
        outer_grad = (scale[:, :, None] * value_heads).astype(jnp.bfloat16).astype(jnp.float32)
        hidden_grad = jnp.einsum('rhj,jhf->rhf', outer_grad, weights[:, 2])
        gate_grad = (hidden_grad * ups * sigma * (1.0 + gates * (1.0 - sigma))).astype(jnp.bfloat16).astype(jnp.float32)
        up_grad = (hidden_grad * active).astype(jnp.bfloat16).astype(jnp.float32)
        grad_gate = jnp.einsum('rhj,rhf->jhf', key_heads, gate_grad)
        grad_up = jnp.einsum('rhj,rhf->jhf', key_heads, up_grad)
        grad_down = jnp.einsum('rhj,rhf->jhf', outer_grad, hidden_act)
        gradient = jnp.stack([grad_gate, grad_up, grad_down], axis=1)
        momentum = 0.9 * momentum + gradient
        state = normalize_rows(state - momentum, initial)
        applied = state.astype(jnp.bfloat16).astype(jnp.float32)
        query_gates, query_ups = forward_heads(query_heads, applied)
        query_hidden = (jax.nn.silu(query_gates) * query_ups).astype(jnp.bfloat16).astype(jnp.float32)
        results.append(jnp.einsum('rhf,jhf->rhj', query_hidden, applied[:, 2]))
    mixed = jnp.where(first[:, None, None], results[0], results[1])
    return mixed.astype(jnp.bfloat16).reshape(TOKENS, HEADS * DK)
```

```python
import functools

import jax
import jax.numpy as jnp
from jax import lax
from jax.experimental import pallas as pl
from jax.experimental.pallas import tpu as pltpu
from jax.sharding import PartitionSpec as P

MOMENTUM_DECAY = 0.9
EPSILON = 1e-06
MESH = pl.DeviceIdType.MESH
BF16 = jnp.bfloat16
F32 = jnp.float32
NY, NC = 2, 2


def dot(lhs, rhs, lhs_dim, rhs_dim):
    return lax.dot_general(
        lhs, rhs, (((lhs_dim,), (rhs_dim,)), ((), ())), preferred_element_type=F32
    )


def step_kernel(
    dims,
    q_hbm, k_hbm, v_hbm, rates_ref, split_ref, init_ref, out_ref,
    q_ref, k_ref, v_ref, w, grad, half, core_in, quarter, y_in, z_in, state, momentum,
    load_sem, agz_s, agz_r, agy_s, agy_r, agc_s, agc_r,
    rsc_s, rsc_r, rsy_s, rsy_r, rsz_s, rsz_r,
):
    heads, rows, width, hidden, nz, owned = dims
    me = lax.axis_index("tok")
    c0 = lax.rem(me, NC)
    y0 = lax.rem(me // NC, NY)
    z0 = me // (NC * NY)
    c1, y1 = 1 - c0, 1 - y0
    z_peers = [lax.rem(z0 + i, nz) for i in range(1, nz)]
    trimmed = rows - rows // 4

    def device(z, y, c):
        return {"tok": (z * NY + y) * NC + c}

    partner, y_peer = device(z0, y0, c1), device(z0, y1, c0)

    def remote(src, dst, send_sem, recv_sem, target):
        return pltpu.make_async_remote_copy(
            src_ref=src, dst_ref=dst, send_sem=send_sem, recv_sem=recv_sem,
            device_id=target, device_id_type=MESH,
        )

    loads = [
        pltpu.make_async_copy(src, dst, load_sem.at[i])
        for i, (src, dst) in enumerate(((k_hbm, k_ref), (v_hbm, v_ref), (q_hbm, q_ref)))
    ]

    def ag_z_copies(r, h):
        mine = w.at[r, h, z0, y0, c0]
        return [
            remote(mine, mine, agz_s.at[r, h, i], agz_r.at[r, h, z0], device(zp, y0, c0))
            for i, zp in enumerate(z_peers)
        ]

    def ag_y_copy(r, h):
        mine = w.at[r, h, :, y0, c0]
        return remote(mine, mine, agy_s.at[r, h], agy_r.at[r, h], y_peer)

    def ag_c_copy(r, h):
        mine = w.at[r, h, :, :, c0]
        return remote(mine, mine, agc_s.at[r, h], agc_r.at[r, h], partner)

    def rs_c_copy(r, h):
        return remote(
            grad.at[r, h, :, :, c1], core_in.at[r, h], rsc_s.at[r, h], rsc_r.at[r, h], partner
        )

    def rs_y_copy(r, h):
        return remote(
            half.at[r, h, :, y1], y_in.at[r, h], rsy_s.at[r, h], rsy_r.at[r, h], y_peer
        )

    def rs_z_copies(r, h):
        return [
            remote(
                quarter.at[r, h, zp], z_in.at[r, h, z0], rsz_s.at[r, h, i], rsz_r.at[r, h, z0],
                device(zp, y0, c0),
            )
            for i, zp in enumerate(z_peers)
        ]

    def ag_z(r, h):
        for copy in ag_z_copies(r, h):
            copy.start()

    def ag_y(r, h):
        for i, zp in enumerate(z_peers):
            there = w.at[r, h, zp, y0, c0]
            remote(there, there, agz_s.at[r, h, i], agz_r.at[r, h, zp], y_peer).wait_recv()
        ag_y_copy(r, h).start()

    def ag_c(r, h):
        there = w.at[r, h, :, y1, c0]
        remote(there, there, agy_s.at[r, h], agy_r.at[r, h], y_peer).wait_recv()
        ag_c_copy(r, h).start()

    def gathered(r, h):
        return w[r, h].reshape(width, 3 * hidden)

    def head_columns(h):
        return pl.ds(pl.multiple_of(h * width, width), width)

    def gradient(r, h):
        there = w.at[r, h, :, :, c1]
        remote(there, there, agc_s.at[r, h], agc_r.at[r, h], partner).wait_recv()
        low = 0 if r == 0 else rows - trimmed
        weights = gathered(r, h)
        keys = k_ref[low : low + trimmed, head_columns(h)]
        values = v_ref[low : low + trimmed, head_columns(h)]
        row = low + lax.broadcasted_iota(jnp.int32, (trimmed, 1), 0)
        first = row < split_ref[0]
        keep = first if r == 0 else jnp.logical_not(first)
        all_rates = rates_ref[low : low + trimmed, :]
        lane = lax.broadcasted_iota(jnp.int32, all_rates.shape, 1)
        rate = jnp.sum(jnp.where(lane == h, all_rates, 0.0), axis=1, keepdims=True)
        scale = -(rate * keep.astype(F32))
        dout = (scale * values.astype(F32)).astype(BF16)
        both = dot(keys, weights[:, : 2 * hidden], 1, 0)
        dhid = dot(dout, weights[:, 2 * hidden :], 1, 0)
        gates, ups = both[:, :hidden], both[:, hidden:]
        sigma = jax.nn.sigmoid(gates)
        active = gates * sigma
        hid = (active * ups).astype(BF16)
        dg = (dhid * ups * sigma * (1.0 + gates * (1.0 - sigma))).astype(BF16)
        du = (dhid * active).astype(BF16)
        to_both = dot(keys, jnp.concatenate([dg, du], axis=1), 0, 0)
        to_down = dot(dout, hid, 0, 0)
        grad[r, h, :, :, :, :, : 2 * hidden] = to_both.astype(BF16).reshape(
            nz, NY, NC, owned, 2 * hidden
        )
        grad[r, h, :, :, :, :, 2 * hidden :] = to_down.astype(BF16).reshape(
            nz, NY, NC, owned, hidden
        )
        rs_c_copy(r, h).start()

    def rs_y(r, h):
        rs_c_copy(r, h).wait_recv()
        half[r, h] = (grad[r, h, :, :, c0].astype(F32) + core_in[r, h].astype(F32)).astype(BF16)
        rs_y_copy(r, h).start()

    def rs_z(r, h):
        rs_y_copy(r, h).wait_recv()
        quarter[r, h] = (half[r, h, :, y0].astype(F32) + y_in[r, h].astype(F32)).astype(BF16)
        for copy in rs_z_copies(r, h):
            copy.start()

    def initial(m, h):
        return init_ref[:, pl.ds(pl.multiple_of((m * heads + h) * hidden, hidden), hidden)]

    def update(r, h):
        total = quarter[r, h, z0].astype(F32)
        for i, zp in enumerate(z_peers):
            there = z_in.at[r, h, zp]
            remote(there, there, rsz_s.at[r, h, i], rsz_r.at[r, h, zp], y_peer).wait_recv()
            total = total + z_in[r, h, zp].astype(F32)
        for m in range(3):
            part = slice(m * hidden, (m + 1) * hidden)
            base = initial(m, h)
            if r == 0:
                moment = total[:, part]
                moved = base - moment
                momentum[h, :, part] = moment
            else:
                moved = state[h, :, part] - (MOMENTUM_DECAY * momentum[h, :, part] + total[:, part])
            target = jnp.sqrt(jnp.mean(base * base, axis=-1, keepdims=True))
            current = jnp.sqrt(jnp.mean(moved * moved, axis=-1, keepdims=True) + EPSILON)
            new = moved * (target / current)
            if r == 0:
                state[h, :, part] = new
            w[r + 1, h, z0, y0, c0, :, part] = new.astype(BF16)
        ag_z(r + 1, h)

    def apply(r, h):
        low = 0 if r == 1 else rows - trimmed
        weights = gathered(r, h)
        queries = q_ref[low : low + trimmed, head_columns(h)]
        both = dot(queries, weights[:, : 2 * hidden], 1, 0)
        gates, ups = both[:, :hidden], both[:, hidden:]
        hid = (gates * jax.nn.sigmoid(gates) * ups).astype(BF16)
        return dot(hid, weights[:, 2 * hidden :], 1, 1).astype(BF16)

    def apply_first(h):
        out_ref[:trimmed, head_columns(h)] = apply(1, h)

    def apply_second(h):
        there = w.at[2, h, :, :, c1]
        remote(there, there, agc_s.at[2, h], agc_r.at[2, h], partner).wait_recv()
        second = apply(2, h)
        low = rows - trimmed
        row = low + lax.broadcasted_iota(jnp.int32, (trimmed - low, 1), 0)
        out_ref[low:trimmed, head_columns(h)] = jnp.where(
            row < split_ref[0],
            out_ref[low:trimmed, head_columns(h)].astype(F32),
            second[: trimmed - low].astype(F32),
        ).astype(BF16)
        out_ref[trimmed:, head_columns(h)] = second[trimmed - low :]

    for load in loads:
        load.start()
    barrier = pltpu.get_barrier_semaphore()
    peers = [partner, y_peer] + [device(zp, y0, c0) for zp in z_peers]
    for peer in peers:
        pl.semaphore_signal(barrier, inc=1, device_id=peer, device_id_type=MESH)
    for h in range(heads):
        for m in range(3):
            w[0, h, z0, y0, c0, :, m * hidden : (m + 1) * hidden] = initial(m, h).astype(BF16)
    pl.semaphore_wait(barrier, len(peers))
    for h in range(heads):
        ag_z(0, h)
    for load in loads:
        load.wait()

    stages = []
    for r in range(2):
        stages += [
            functools.partial(stage, r) for stage in (ag_y, ag_c, gradient, rs_y, rs_z, update)
        ]
    stages += [functools.partial(ag_y, 2), functools.partial(ag_c, 2), apply_second]
    order = [(s, stages[s]) for s in reversed(range(len(stages)))] + [(9, apply_first)]

    def tick(t, carry):
        for s, stage in order:
            h = t - s

            @pl.when(jnp.logical_and(h >= 0, h < heads))
            def _():
                stage(h)

        return carry

    lax.fori_loop(0, len(stages) + heads - 1, tick, 0)

    def drain(h, carry):
        for r in range(3):
            for copy in ag_z_copies(r, h) + [ag_y_copy(r, h), ag_c_copy(r, h)]:
                copy.wait_send()
        for r in range(2):
            for copy in [rs_c_copy(r, h), rs_y_copy(r, h)] + rs_z_copies(r, h):
                copy.wait_send()
        return carry

    lax.fori_loop(0, heads, drain, 0)


def fused_step(queries, keys, values, rates, split_row, fast_init):
    rows, features = queries.shape
    heads = rates.shape[1]
    width = features // heads
    hidden = fast_init.shape[1] // (3 * heads)
    owned = fast_init.shape[0]
    nz = lax.axis_size("tok") // (NY * NC)
    chunk = (owned, 3 * hidden)
    hbm = pl.BlockSpec(memory_space=pl.ANY)
    vmem = pl.BlockSpec(memory_space=pltpu.VMEM)
    dma = pltpu.SemaphoreType.DMA
    return pl.pallas_call(
        functools.partial(step_kernel, (heads, rows, width, hidden, nz, owned)),
        out_shape=jax.ShapeDtypeStruct((rows, features), BF16),
        in_specs=[hbm, hbm, hbm, vmem, pl.BlockSpec(memory_space=pltpu.SMEM), vmem],
        out_specs=vmem,
        scratch_shapes=[
            pltpu.VMEM((rows, features), BF16),
            pltpu.VMEM((rows, features), BF16),
            pltpu.VMEM((rows, features), BF16),
            pltpu.VMEM((3, heads, nz, NY, NC) + chunk, BF16),
            pltpu.VMEM((2, heads, nz, NY, NC) + chunk, BF16),
            pltpu.VMEM((2, heads, nz, NY) + chunk, BF16),
            pltpu.VMEM((2, heads, nz, NY) + chunk, BF16),
            pltpu.VMEM((2, heads, nz) + chunk, BF16),
            pltpu.VMEM((2, heads, nz) + chunk, BF16),
            pltpu.VMEM((2, heads, nz) + chunk, BF16),
            pltpu.VMEM((heads,) + chunk, F32),
            pltpu.VMEM((heads,) + chunk, F32),
            dma((3,)),
            dma((3, heads, nz - 1)),
            dma((3, heads, nz)),
            dma((3, heads)),
            dma((3, heads)),
            dma((3, heads)),
            dma((3, heads)),
            dma((2, heads)),
            dma((2, heads)),
            dma((2, heads)),
            dma((2, heads)),
            dma((2, heads, nz - 1)),
            dma((2, heads, nz)),
        ],
        compiler_params=pltpu.CompilerParams(
            collective_id=0, has_side_effects=True, vmem_limit_bytes=60 * 1024 * 1024
        ),
        name="fast_weight_step",
    )(queries, keys, values, rates, split_row, fast_init)


def gather_weights(shard, heads, hidden):
    gathered = lax.all_gather(shard, "tok", axis=0, tiled=True)
    return gathered.reshape(gathered.shape[0], 3, heads, hidden)


def products(stacked, gathered):
    gates = jnp.einsum("rhj,jhf->rhf", stacked, gathered[:, 0], preferred_element_type=jnp.float32)
    ups = jnp.einsum("rhj,jhf->rhf", stacked, gathered[:, 1], preferred_element_type=jnp.float32)
    return (gates, ups)


def segment_gradient(key_heads, value_heads, rates, keep, gates, ups, down, owned_rows):
    sigma = jax.nn.sigmoid(gates)
    active = gates * sigma
    hidden_act = (active * ups).astype(jnp.bfloat16)
    scale = -(rates * keep[:, None].astype(jnp.float32))
    outer_grad = (scale[:, :, None] * value_heads.astype(jnp.float32)).astype(jnp.bfloat16)
    hidden_grad = jnp.einsum("rhj,jhf->rhf", outer_grad, down, preferred_element_type=jnp.float32)
    backward_gate_grad = (hidden_grad * ups * sigma * (1.0 + gates * (1.0 - sigma))).astype(
        jnp.bfloat16
    )
    backward_up_grad = (hidden_grad * active).astype(jnp.bfloat16)
    grad_gate = jnp.einsum(
        "rhj,rhf->jhf", key_heads, backward_gate_grad, preferred_element_type=jnp.float32
    )
    grad_up = jnp.einsum(
        "rhj,rhf->jhf", key_heads, backward_up_grad, preferred_element_type=jnp.float32
    )
    grad_gate, grad_up = (grad_gate, grad_up)
    grad_down = jnp.einsum(
        "rhj,rhf->jhf", outer_grad, hidden_act, preferred_element_type=jnp.float32
    )
    return lax.psum_scatter(
        jnp.stack([grad_gate, grad_up, grad_down], axis=1).reshape(
            lax.axis_size("tok") * owned_rows, -1
        ),
        "tok",
        scatter_dimension=0,
        tiled=True,
    )


def owner_update(state, momentum, gradient, initial, heads, hidden):
    momentum = MOMENTUM_DECAY * momentum + gradient
    moved = (state - momentum).reshape(state.shape[0], 3 * heads, hidden)
    base = initial.reshape(state.shape[0], 3 * heads, hidden)
    target = jnp.sqrt(jnp.mean(base * base, axis=-1, keepdims=True))
    current = jnp.sqrt(jnp.mean(moved * moved, axis=-1, keepdims=True) + EPSILON)
    return ((moved * (target / current)).reshape(state.shape), momentum)


def apply_fast(gates, ups, down):
    query_hidden = (jax.nn.silu(gates) * ups).astype(jnp.bfloat16)
    return jnp.einsum("rhf,jhf->rhj", query_hidden, down, preferred_element_type=jnp.float32)


def per_device(queries, keys, values, rates, split_row, fast_init):
    token_rows = queries.shape[0]
    heads = rates.shape[1]
    width = queries.shape[1] // heads
    hidden = fast_init.shape[1] // (3 * heads)
    owned_rows = fast_init.shape[0]
    query_heads = queries.reshape(token_rows, heads, width)
    key_heads = keys.reshape(token_rows, heads, width)
    value_heads = values.reshape(token_rows, heads, width)
    first = jnp.arange(token_rows) < split_row[0]
    second = jnp.logical_not(first)
    momentum = jnp.zeros_like(fast_init)
    gathered = gather_weights(fast_init.astype(jnp.bfloat16), heads, hidden)
    gates, ups = products(key_heads, gathered)
    gradient = segment_gradient(
        key_heads, value_heads, rates, first, gates, ups, gathered[:, 2], owned_rows
    )
    state, momentum = owner_update(fast_init, momentum, gradient, fast_init, heads, hidden)
    gathered = gather_weights(state.astype(jnp.bfloat16), heads, hidden)
    down = gathered[:, 2]
    stacked = jnp.concatenate([query_heads, key_heads], axis=0)
    gates, ups = products(stacked, gathered)
    out_first = apply_fast(gates[:token_rows], ups[:token_rows], down)
    gradient = segment_gradient(
        key_heads,
        value_heads,
        rates,
        second,
        gates[token_rows:],
        ups[token_rows:],
        down,
        owned_rows,
    )
    state, momentum = owner_update(state, momentum, gradient, fast_init, heads, hidden)
    gathered = gather_weights(state.astype(jnp.bfloat16), heads, hidden)
    gates, ups = products(query_heads, gathered)
    out_second = apply_fast(gates, ups, gathered[:, 2])
    mixed = jnp.where(first[:, None, None], out_first, out_second)
    return mixed.astype(jnp.bfloat16).reshape(token_rows, heads * width)


def plan(*args):
    size = lax.axis_size("tok")
    small = size // (NY * NC) in (2, 3, 4) and size % (NY * NC) == 0
    if small and args[5].shape[0] % 16 == 0:
        return fused_step(*args)
    return per_device(*args)


def solution(mesh):
    in_specs = (
        P(("groups", "tok"), None),
        P(("groups", "tok"), None),
        P(("groups", "tok"), None),
        P(("groups", "tok"), None),
        P(("groups", "tok")),
        P("tok", None),
    )
    out_specs = P(("groups", "tok"), None)
    return jax.shard_map(
        plan, mesh=mesh, in_specs=in_specs, out_specs=out_specs, check_vma=False
    )
```

```python
import functools

import jax
import jax.numpy as jnp
from jax import lax
from jax.experimental import pallas as pl
from jax.experimental.pallas import tpu as pltpu
from jax.sharding import PartitionSpec as P

MOMENTUM_DECAY = 0.9
EPSILON = 1e-06
MESH = pl.DeviceIdType.MESH
BF16 = jnp.bfloat16
F32 = jnp.float32
NY, NC = 2, 2


def dot(lhs, rhs, lhs_dim, rhs_dim):
    return lax.dot_general(
        lhs, rhs, (((lhs_dim,), (rhs_dim,)), ((), ())), preferred_element_type=F32
    )


def step_kernel(
    dims,
    q_hbm, k_hbm, v_hbm, rates_ref, split_ref, init_ref, out_ref,
    q_ref, k_ref, v_ref, w, own, grad, half, core_in, quarter, y_in, z_in, state, momentum,
    load_sem, agz_s, agz_r, agy_s, agy_r, agc_s, agc_r,
    rsc_s, rsc_r, rsy_s, rsy_r, rsz_s, rsz_r,
):
    heads, rows, width, hidden, nz, owned = dims
    me = lax.axis_index("tok")
    c0 = lax.rem(me, NC)
    y0 = lax.rem(me // NC, NY)
    z0 = me // (NC * NY)
    c1, y1 = 1 - c0, 1 - y0
    z_peers = [lax.rem(z0 + i, nz) for i in range(1, nz)]
    trimmed = rows - rows // 4

    def device(z, y, c):
        return {"tok": (z * NY + y) * NC + c}

    partner, y_peer = device(z0, y0, c1), device(z0, y1, c0)

    def remote(src, dst, send_sem, recv_sem, target):
        return pltpu.make_async_remote_copy(
            src_ref=src, dst_ref=dst, send_sem=send_sem, recv_sem=recv_sem,
            device_id=target, device_id_type=MESH,
        )

    loads = [
        pltpu.make_async_copy(src, dst, load_sem.at[i])
        for i, (src, dst) in enumerate(((k_hbm, k_ref), (v_hbm, v_ref), (q_hbm, q_ref)))
    ]

    def ag_z_copies(r, h):
        mine = w.at[r, h, z0, y0, c0]
        return [
            remote(mine, mine, agz_s.at[r, h, i], agz_r.at[r, h, z0], device(zp, y0, c0))
            for i, zp in enumerate(z_peers)
        ]

    def ag_y_copy(r, h, z):
        mine = w.at[r, h, z, y0, c0]
        return remote(mine, mine, agy_s.at[r, h, z], agy_r.at[r, h, z], y_peer)

    def ag_c_copy(r, h, y):
        mine = w.at[r, h, :, y, c0]
        return remote(mine, mine, agc_s.at[r, h, y], agc_r.at[r, h, y], partner)

    def rs_c_copy(r, h, y):
        return remote(
            grad.at[r, h, :, y, c1], core_in.at[r, h, :, y],
            rsc_s.at[r, h, y], rsc_r.at[r, h, y], partner,
        )

    def rs_y_copy(r, h, z):
        return remote(
            half.at[r, h, z], y_in.at[r, h, z], rsy_s.at[r, h, z], rsy_r.at[r, h, z], y_peer
        )

    def rs_z_copies(r, h):
        return [
            remote(
                quarter.at[r, h, zp], z_in.at[r, h, z0], rsz_s.at[r, h, i], rsz_r.at[r, h, z0],
                device(zp, y0, c0),
            )
            for i, zp in enumerate(z_peers)
        ]

    def ag_z(r, h):
        for copy in ag_z_copies(r, h):
            copy.start()
        ag_y_copy(r, h, z0).start()

    def ag_y(r, h):
        for i, zp in enumerate(z_peers):
            there = w.at[r, h, zp, y0, c0]
            remote(there, there, agz_s.at[r, h, i], agz_r.at[r, h, zp], y_peer).wait_recv()
            ag_y_copy(r, h, zp).start()
        ag_c_copy(r, h, y0).start()

    def ag_c(r, h):
        for z in range(nz):
            there = w.at[r, h, z, y1, c0]
            remote(there, there, agy_s.at[r, h, z], agy_r.at[r, h, z], y_peer).wait_recv()
        ag_c_copy(r, h, y1).start()

    def ag_wait(r, h):
        for y in range(NY):
            there = w.at[r, h, :, y, c1]
            remote(there, there, agc_s.at[r, h, y], agc_r.at[r, h, y], partner).wait_recv()

    def gathered(r, h):
        return w[r, h].reshape(width, 3 * hidden)

    def head_columns(h):
        return pl.ds(pl.multiple_of(h * width, width), width)

    def gradient(r, h):
        ag_wait(r, h)
        low = 0 if r == 0 else rows - trimmed
        weights = gathered(r, h)
        keys = k_ref[low : low + trimmed, head_columns(h)]
        values = v_ref[low : low + trimmed, head_columns(h)]
        row = low + lax.broadcasted_iota(jnp.int32, (trimmed, 1), 0)
        first = row < split_ref[0]
        keep = first if r == 0 else jnp.logical_not(first)
        across = lax.broadcasted_iota(jnp.int32, (trimmed, trimmed), 0)
        along = lax.broadcasted_iota(jnp.int32, (trimmed, trimmed), 1)
        rate_row = rates_ref[pl.ds(h, 1), low : low + trimmed]
        rate = jnp.sum(jnp.where(across == along, rate_row, 0.0), axis=1, keepdims=True)
        scale = -(rate * keep.astype(F32))
        dout = (scale * values.astype(F32)).astype(BF16)
        both = dot(keys, weights[:, : 2 * hidden], 1, 0)
        dhid = dot(dout, weights[:, 2 * hidden :], 1, 0)
        gates, ups = both[:, :hidden], both[:, hidden:]
        sigma = jax.nn.sigmoid(gates)
        active = gates * sigma
        hid = (active * ups).astype(BF16)
        dg = (dhid * ups * sigma * (1.0 + gates * (1.0 - sigma))).astype(BF16)
        du = (dhid * active).astype(BF16)
        to_both = dot(keys, jnp.concatenate([dg, du], axis=1), 0, 0)
        to_down = dot(dout, hid, 0, 0)
        to_both = to_both.reshape(nz, NY, NC, owned, 2 * hidden)
        to_down = to_down.reshape(nz, NY, NC, owned, hidden)
        grad[r, h, :, :, :, :, : 2 * hidden] = to_both.astype(BF16)
        grad[r, h, :, :, :, :, 2 * hidden :] = to_down.astype(BF16)
        rs_c_copy(r, h, y1).start()
        rs_c_copy(r, h, y0).start()
        own[h, :, :, :, :, : 2 * hidden] = to_both
        own[h, :, :, :, :, 2 * hidden :] = to_down

    def rs_y(r, h):
        rs_c_copy(r, h, y1).wait_recv()
        for z in z_peers + [z0]:
            half[r, h, z] = (own[h, z, y1, c0] + core_in[r, h, z, y1].astype(F32)).astype(BF16)
            rs_y_copy(r, h, z).start()

    def pair_sum(r, h, z):
        rs_y_copy(r, h, z).wait_recv()
        return own[h, z, y0, c0] + core_in[r, h, z, y0].astype(F32) + y_in[r, h, z].astype(F32)

    def rs_z(r, h):
        rs_c_copy(r, h, y0).wait_recv()
        for zp, copy in zip(z_peers, rs_z_copies(r, h)):
            quarter[r, h, zp] = pair_sum(r, h, zp).astype(BF16)
            copy.start()

    def initial(m, h):
        return init_ref[:, pl.ds(pl.multiple_of((m * heads + h) * hidden, hidden), hidden)]

    def update(r, h):
        total = pair_sum(r, h, z0)
        for i, zp in enumerate(z_peers):
            there = z_in.at[r, h, zp]
            remote(there, there, rsz_s.at[r, h, i], rsz_r.at[r, h, zp], y_peer).wait_recv()
            total = total + z_in[r, h, zp].astype(F32)
        for m in range(3):
            part = slice(m * hidden, (m + 1) * hidden)
            base = initial(m, h)
            if r == 0:
                moment = total[:, part]
                moved = base - moment
                momentum[h, :, part] = moment
            else:
                moved = state[h, :, part] - (MOMENTUM_DECAY * momentum[h, :, part] + total[:, part])
            target = jnp.sqrt(jnp.mean(base * base, axis=-1, keepdims=True))
            current = jnp.sqrt(jnp.mean(moved * moved, axis=-1, keepdims=True) + EPSILON)
            new = moved * (target / current)
            if r == 0:
                state[h, :, part] = new
            w[r + 1, h, z0, y0, c0, :, part] = new.astype(BF16)
        ag_z(r + 1, h)

    def apply(r, h):
        low = 0 if r == 1 else rows - trimmed
        weights = gathered(r, h)
        queries = q_ref[low : low + trimmed, head_columns(h)]
        both = dot(queries, weights[:, : 2 * hidden], 1, 0)
        gates, ups = both[:, :hidden], both[:, hidden:]
        hid = (gates * jax.nn.sigmoid(gates) * ups).astype(BF16)
        return dot(hid, weights[:, 2 * hidden :], 1, 1).astype(BF16)

    def apply_first(h):
        out_ref[:trimmed, head_columns(h)] = apply(1, h)

    def apply_second(h):
        ag_wait(2, h)
        second = apply(2, h)
        low = rows - trimmed
        row = low + lax.broadcasted_iota(jnp.int32, (trimmed - low, 1), 0)
        out_ref[low:trimmed, head_columns(h)] = jnp.where(
            row < split_ref[0],
            out_ref[low:trimmed, head_columns(h)].astype(F32),
            second[: trimmed - low].astype(F32),
        ).astype(BF16)
        out_ref[trimmed:, head_columns(h)] = second[trimmed - low :]

    for load in loads:
        load.start()
    barrier = pltpu.get_barrier_semaphore()
    peers = [partner, y_peer] + [device(zp, y0, c0) for zp in z_peers]
    for peer in peers:
        pl.semaphore_signal(barrier, inc=1, device_id=peer, device_id_type=MESH)
    for h in range(heads):
        for m in range(3):
            w[0, h, z0, y0, c0, :, m * hidden : (m + 1) * hidden] = initial(m, h).astype(BF16)
    pl.semaphore_wait(barrier, len(peers))
    for h in range(heads):
        ag_z(0, h)
    for load in loads:
        load.wait()

    stages = []
    for r in range(2):
        stages += [
            functools.partial(stage, r) for stage in (ag_y, ag_c, gradient, rs_y, rs_z, update)
        ]
    stages += [functools.partial(ag_y, 2), functools.partial(ag_c, 2), apply_second]
    order = [(s, stages[s]) for s in reversed(range(len(stages)))] + [(9, apply_first)]

    def tick(t, carry):
        for s, stage in order:
            h = t - s

            @pl.when(jnp.logical_and(h >= 0, h < heads))
            def _():
                stage(h)

        return carry

    lax.fori_loop(0, len(stages) + heads - 1, tick, 0)

    def drain(h, carry):
        for r in range(3):
            along_y = [ag_y_copy(r, h, z) for z in range(nz)]
            for copy in ag_z_copies(r, h) + along_y + [ag_c_copy(r, h, y) for y in range(NY)]:
                copy.wait_send()
        for r in range(2):
            along_y = [rs_y_copy(r, h, z) for z in range(nz)]
            for copy in rs_z_copies(r, h) + along_y + [rs_c_copy(r, h, y) for y in range(NY)]:
                copy.wait_send()
        return carry

    lax.fori_loop(0, heads, drain, 0)


def fused_step(queries, keys, values, rates, split_row, fast_init):
    rows, features = queries.shape
    heads = rates.shape[1]
    width = features // heads
    hidden = fast_init.shape[1] // (3 * heads)
    owned = fast_init.shape[0]
    nz = lax.axis_size("tok") // (NY * NC)
    chunk = (owned, 3 * hidden)
    hbm = pl.BlockSpec(memory_space=pl.ANY)
    vmem = pl.BlockSpec(memory_space=pltpu.VMEM)
    dma = pltpu.SemaphoreType.DMA
    return pl.pallas_call(
        functools.partial(step_kernel, (heads, rows, width, hidden, nz, owned)),
        out_shape=jax.ShapeDtypeStruct((rows, features), BF16),
        in_specs=[hbm, hbm, hbm, vmem, pl.BlockSpec(memory_space=pltpu.SMEM), vmem],
        out_specs=vmem,
        scratch_shapes=[
            pltpu.VMEM((rows, features), BF16),
            pltpu.VMEM((rows, features), BF16),
            pltpu.VMEM((rows, features), BF16),
            pltpu.VMEM((3, heads, nz, NY, NC) + chunk, BF16),
            pltpu.VMEM((heads, nz, NY, NC) + chunk, F32),
            pltpu.VMEM((2, heads, nz, NY, NC) + chunk, BF16),
            pltpu.VMEM((2, heads, nz) + chunk, BF16),
            pltpu.VMEM((2, heads, nz, NY) + chunk, BF16),
            pltpu.VMEM((2, heads, nz) + chunk, BF16),
            pltpu.VMEM((2, heads, nz) + chunk, BF16),
            pltpu.VMEM((2, heads, nz) + chunk, BF16),
            pltpu.VMEM((heads,) + chunk, F32),
            pltpu.VMEM((heads,) + chunk, F32),
            dma((3,)),
            dma((3, heads, nz - 1)),
            dma((3, heads, nz)),
            dma((3, heads, nz)),
            dma((3, heads, nz)),
            dma((3, heads, NY)),
            dma((3, heads, NY)),
            dma((2, heads, NY)),
            dma((2, heads, NY)),
            dma((2, heads, nz)),
            dma((2, heads, nz)),
            dma((2, heads, nz - 1)),
            dma((2, heads, nz)),
        ],
        compiler_params=pltpu.CompilerParams(
            collective_id=0, has_side_effects=True, vmem_limit_bytes=60 * 1024 * 1024
        ),
        name="fast_weight_step",
    )(queries, keys, values, rates.T, split_row, fast_init)


def gather_weights(shard, heads, hidden):
    gathered = lax.all_gather(shard, "tok", axis=0, tiled=True)
    return gathered.reshape(gathered.shape[0], 3, heads, hidden)


def products(stacked, gathered):
    gates = jnp.einsum("rhj,jhf->rhf", stacked, gathered[:, 0], preferred_element_type=jnp.float32)
    ups = jnp.einsum("rhj,jhf->rhf", stacked, gathered[:, 1], preferred_element_type=jnp.float32)
    return (gates, ups)


def segment_gradient(key_heads, value_heads, rates, keep, gates, ups, down, owned_rows):
    sigma = jax.nn.sigmoid(gates)
    active = gates * sigma
    hidden_act = (active * ups).astype(jnp.bfloat16)
    scale = -(rates * keep[:, None].astype(jnp.float32))
    outer_grad = (scale[:, :, None] * value_heads.astype(jnp.float32)).astype(jnp.bfloat16)
    hidden_grad = jnp.einsum("rhj,jhf->rhf", outer_grad, down, preferred_element_type=jnp.float32)
    backward_gate_grad = (hidden_grad * ups * sigma * (1.0 + gates * (1.0 - sigma))).astype(
        jnp.bfloat16
    )
    backward_up_grad = (hidden_grad * active).astype(jnp.bfloat16)
    grad_gate = jnp.einsum(
        "rhj,rhf->jhf", key_heads, backward_gate_grad, preferred_element_type=jnp.float32
    )
    grad_up = jnp.einsum(
        "rhj,rhf->jhf", key_heads, backward_up_grad, preferred_element_type=jnp.float32
    )
    grad_gate, grad_up = (grad_gate, grad_up)
    grad_down = jnp.einsum(
        "rhj,rhf->jhf", outer_grad, hidden_act, preferred_element_type=jnp.float32
    )
    return lax.psum_scatter(
        jnp.stack([grad_gate, grad_up, grad_down], axis=1).reshape(
            lax.axis_size("tok") * owned_rows, -1
        ),
        "tok",
        scatter_dimension=0,
        tiled=True,
    )


def owner_update(state, momentum, gradient, initial, heads, hidden):
    momentum = MOMENTUM_DECAY * momentum + gradient
    moved = (state - momentum).reshape(state.shape[0], 3 * heads, hidden)
    base = initial.reshape(state.shape[0], 3 * heads, hidden)
    target = jnp.sqrt(jnp.mean(base * base, axis=-1, keepdims=True))
    current = jnp.sqrt(jnp.mean(moved * moved, axis=-1, keepdims=True) + EPSILON)
    return ((moved * (target / current)).reshape(state.shape), momentum)


def apply_fast(gates, ups, down):
    query_hidden = (jax.nn.silu(gates) * ups).astype(jnp.bfloat16)
    return jnp.einsum("rhf,jhf->rhj", query_hidden, down, preferred_element_type=jnp.float32)


def per_device(queries, keys, values, rates, split_row, fast_init):
    token_rows = queries.shape[0]
    heads = rates.shape[1]
    width = queries.shape[1] // heads
    hidden = fast_init.shape[1] // (3 * heads)
    owned_rows = fast_init.shape[0]
    query_heads = queries.reshape(token_rows, heads, width)
    key_heads = keys.reshape(token_rows, heads, width)
    value_heads = values.reshape(token_rows, heads, width)
    first = jnp.arange(token_rows) < split_row[0]
    second = jnp.logical_not(first)
    momentum = jnp.zeros_like(fast_init)
    gathered = gather_weights(fast_init.astype(jnp.bfloat16), heads, hidden)
    gates, ups = products(key_heads, gathered)
    gradient = segment_gradient(
        key_heads, value_heads, rates, first, gates, ups, gathered[:, 2], owned_rows
    )
    state, momentum = owner_update(fast_init, momentum, gradient, fast_init, heads, hidden)
    gathered = gather_weights(state.astype(jnp.bfloat16), heads, hidden)
    down = gathered[:, 2]
    stacked = jnp.concatenate([query_heads, key_heads], axis=0)
    gates, ups = products(stacked, gathered)
    out_first = apply_fast(gates[:token_rows], ups[:token_rows], down)
    gradient = segment_gradient(
        key_heads,
        value_heads,
        rates,
        second,
        gates[token_rows:],
        ups[token_rows:],
        down,
        owned_rows,
    )
    state, momentum = owner_update(state, momentum, gradient, fast_init, heads, hidden)
    gathered = gather_weights(state.astype(jnp.bfloat16), heads, hidden)
    gates, ups = products(query_heads, gathered)
    out_second = apply_fast(gates, ups, gathered[:, 2])
    mixed = jnp.where(first[:, None, None], out_first, out_second)
    return mixed.astype(jnp.bfloat16).reshape(token_rows, heads * width)


def plan(*args):
    size = lax.axis_size("tok")
    small = size // (NY * NC) in (2, 3, 4) and size % (NY * NC) == 0
    if small and args[5].shape[0] % 16 == 0:
        return fused_step(*args)
    return per_device(*args)


def solution(mesh):
    in_specs = (
        P(("groups", "tok"), None),
        P(("groups", "tok"), None),
        P(("groups", "tok"), None),
        P(("groups", "tok"), None),
        P(("groups", "tok")),
        P("tok", None),
    )
    out_specs = P(("groups", "tok"), None)
    return jax.shard_map(
        plan, mesh=mesh, in_specs=in_specs, out_specs=out_specs, check_vma=False
    )
```

```python
import functools

import jax
import jax.numpy as jnp
from jax import lax
from jax.experimental import pallas as pl
from jax.experimental.pallas import tpu as pltpu
from jax.sharding import PartitionSpec as P

MOMENTUM_DECAY = 0.9
EPSILON = 1e-06
MESH = pl.DeviceIdType.MESH
BF16 = jnp.bfloat16
F32 = jnp.float32
NY, NC = 2, 2


def dot(lhs, rhs, lhs_dim, rhs_dim):
    return lax.dot_general(
        lhs, rhs, (((lhs_dim,), (rhs_dim,)), ((), ())), preferred_element_type=F32
    )


def step_kernel(
    dims,
    q_hbm, k_hbm, v_hbm, rates_ref, split_ref, init_ref, out_ref,
    q_ref, k_ref, v_ref, w, own, grad, half, core_in, quarter, y_in, z_in, state, momentum,
    load_sem, agz_s, agz_r, agy_s, agy_r, agc_s, agc_r, agx_s, agx_r,
    rsc_s, rsc_r, rsy_s, rsy_r, rsz_s, rsz_r,
):
    heads, rows, width, hidden, nz, owned = dims
    me = lax.axis_index("tok")
    g0 = lax.axis_index("groups")
    c0 = lax.rem(me, NC)
    y0 = lax.rem(me // NC, NY)
    z0 = me // (NC * NY)
    c1, y1 = 1 - c0, 1 - y0
    z_peers = [lax.rem(z0 + i, nz) for i in range(1, nz)]
    trimmed = rows - rows // 4

    def device(z, y, c):
        return {"tok": (z * NY + y) * NC + c}

    x_peer = {"groups": 1 - g0}
    gathered_here = pl.ds(pl.multiple_of(g0 * hidden, hidden), 2 * hidden)
    sent_across = pl.ds(pl.multiple_of(g0 * 2 * hidden, hidden), hidden)
    got_across = pl.ds(pl.multiple_of((1 - g0) * 2 * hidden, hidden), hidden)

    partner, y_peer = device(z0, y0, c1), device(z0, y1, c0)

    def remote(src, dst, send_sem, recv_sem, target):
        return pltpu.make_async_remote_copy(
            src_ref=src, dst_ref=dst, send_sem=send_sem, recv_sem=recv_sem,
            device_id=target, device_id_type=MESH,
        )

    loads = [
        pltpu.make_async_copy(src, dst, load_sem.at[i])
        for i, (src, dst) in enumerate(((k_hbm, k_ref), (v_hbm, v_ref), (q_hbm, q_ref)))
    ]

    def shard(r, h, z, y):
        if r == 0:
            return w.at[r, h, z, y, c0, :, gathered_here]
        return w.at[r, h, z, y, c0]

    def ag_x_copy(h, z, y):
        part = w.at[0, h, z, y, c0, :, sent_across]
        return remote(part, part, agx_s.at[h, z, y], agx_r.at[h, z, y], x_peer)

    def ag_z_copies(r, h):
        mine = shard(r, h, z0, y0)
        return [
            remote(mine, mine, agz_s.at[r, h, i], agz_r.at[r, h, z0], device(zp, y0, c0))
            for i, zp in enumerate(z_peers)
        ]

    def ag_y_copy(r, h, z):
        mine = shard(r, h, z, y0)
        return remote(mine, mine, agy_s.at[r, h, z], agy_r.at[r, h, z], y_peer)

    def ag_c_copy(r, h, y):
        mine = w.at[r, h, :, y, c0]
        return remote(mine, mine, agc_s.at[r, h, y], agc_r.at[r, h, y], partner)

    def rs_c_copy(r, h, y):
        return remote(
            grad.at[r, h, :, y, c1], core_in.at[r, h, :, y],
            rsc_s.at[r, h, y], rsc_r.at[r, h, y], partner,
        )

    def rs_y_copy(r, h, z):
        return remote(
            half.at[r, h, z], y_in.at[r, h, z], rsy_s.at[r, h, z], rsy_r.at[r, h, z], y_peer
        )

    def rs_z_copies(r, h):
        return [
            remote(
                quarter.at[r, h, zp], z_in.at[r, h, z0], rsz_s.at[r, h, i], rsz_r.at[r, h, z0],
                device(zp, y0, c0),
            )
            for i, zp in enumerate(z_peers)
        ]

    def ag_z(r, h):
        for copy in ag_z_copies(r, h):
            copy.start()
        ag_y_copy(r, h, z0).start()

    def ag_y(r, h):
        for i, zp in reversed(list(enumerate(z_peers))):
            there = shard(r, h, zp, y0)
            remote(there, there, agz_s.at[r, h, i], agz_r.at[r, h, zp], y_peer).wait_recv()
            ag_y_copy(r, h, zp).start()
            if r == 0:
                ag_x_copy(h, zp, y0).start()
        if r > 0:
            ag_c_copy(r, h, y0).start()

    def ag_c(r, h):
        for z in [z0] + z_peers[::-1]:
            there = shard(r, h, z, y1)
            remote(there, there, agy_s.at[r, h, z], agy_r.at[r, h, z], y_peer).wait_recv()
            if r == 0:
                ag_x_copy(h, z, y1).start()
        if r > 0:
            ag_c_copy(r, h, y1).start()

    def ag_x(h):
        for y, zs in ((y0, z_peers[::-1]), (y1, [z0] + z_peers[::-1])):
            for z in zs:
                there = w.at[0, h, z, y, c0, :, got_across]
                remote(there, there, agx_s.at[h, z, y], agx_r.at[h, z, y], x_peer).wait_recv()
            ag_c_copy(0, h, y).start()

    def ag_wait(r, h):
        for y in range(NY):
            there = w.at[r, h, :, y, c1]
            remote(there, there, agc_s.at[r, h, y], agc_r.at[r, h, y], partner).wait_recv()

    def gathered(r, h):
        return w[r, h].reshape(width, 3 * hidden)

    def head_columns(h):
        return pl.ds(pl.multiple_of(h * width, width), width)

    def gradient(r, h):
        ag_wait(r, h)
        low = 0 if r == 0 else rows - trimmed
        weights = gathered(r, h)
        keys = k_ref[low : low + trimmed, head_columns(h)]
        values = v_ref[low : low + trimmed, head_columns(h)]
        row = low + lax.broadcasted_iota(jnp.int32, (trimmed, 1), 0)
        first = row < split_ref[0]
        keep = first if r == 0 else jnp.logical_not(first)
        across = lax.broadcasted_iota(jnp.int32, (trimmed, trimmed), 0)
        along = lax.broadcasted_iota(jnp.int32, (trimmed, trimmed), 1)
        rate_row = rates_ref[pl.ds(h, 1), low : low + trimmed]
        rate = jnp.sum(jnp.where(across == along, rate_row, 0.0), axis=1, keepdims=True)
        scale = -(rate * keep.astype(F32))
        dout = (scale * values.astype(F32)).astype(BF16)
        both = dot(keys, weights[:, : 2 * hidden], 1, 0)
        dhid = dot(dout, weights[:, 2 * hidden :], 1, 0)
        gates, ups = both[:, :hidden], both[:, hidden:]
        sigma = jax.nn.sigmoid(gates)
        active = gates * sigma
        hid = (active * ups).astype(BF16)
        dg = (dhid * ups * sigma * (1.0 + gates * (1.0 - sigma))).astype(BF16)
        du = (dhid * active).astype(BF16)
        to_both = dot(keys, jnp.concatenate([dg, du], axis=1), 0, 0)
        to_down = dot(dout, hid, 0, 0)
        to_both = to_both.reshape(nz, NY, NC, owned, 2 * hidden)
        to_down = to_down.reshape(nz, NY, NC, owned, hidden)
        grad[r, h, :, :, :, :, : 2 * hidden] = to_both.astype(BF16)
        grad[r, h, :, :, :, :, 2 * hidden :] = to_down.astype(BF16)
        rs_c_copy(r, h, y1).start()
        rs_c_copy(r, h, y0).start()
        own[h, :, :, :, :, : 2 * hidden] = to_both
        own[h, :, :, :, :, 2 * hidden :] = to_down

    def rs_y(r, h):
        rs_c_copy(r, h, y1).wait_recv()
        for z in z_peers + [z0]:
            half[r, h, z] = (own[h, z, y1, c0] + core_in[r, h, z, y1].astype(F32)).astype(BF16)
            rs_y_copy(r, h, z).start()

    def pair_sum(r, h, z):
        rs_y_copy(r, h, z).wait_recv()
        return own[h, z, y0, c0] + core_in[r, h, z, y0].astype(F32) + y_in[r, h, z].astype(F32)

    def rs_z(r, h):
        rs_c_copy(r, h, y0).wait_recv()
        for zp, copy in zip(z_peers, rs_z_copies(r, h)):
            quarter[r, h, zp] = pair_sum(r, h, zp).astype(BF16)
            copy.start()

    def initial(m, h):
        return init_ref[:, pl.ds(pl.multiple_of((m * heads + h) * hidden, hidden), hidden)]

    def update(r, h):
        total = pair_sum(r, h, z0)
        for i, zp in enumerate(z_peers):
            there = z_in.at[r, h, zp]
            remote(there, there, rsz_s.at[r, h, i], rsz_r.at[r, h, zp], y_peer).wait_recv()
            total = total + z_in[r, h, zp].astype(F32)
        for m in range(3):
            part = slice(m * hidden, (m + 1) * hidden)
            base = initial(m, h)
            if r == 0:
                moment = total[:, part]
                moved = base - moment
                momentum[h, :, part] = moment
            else:
                moved = state[h, :, part] - (MOMENTUM_DECAY * momentum[h, :, part] + total[:, part])
            target = jnp.sqrt(jnp.mean(base * base, axis=-1, keepdims=True))
            current = jnp.sqrt(jnp.mean(moved * moved, axis=-1, keepdims=True) + EPSILON)
            new = moved * (target / current)
            if r == 0:
                state[h, :, part] = new
            w[r + 1, h, z0, y0, c0, :, part] = new.astype(BF16)
        ag_z(r + 1, h)

    def apply(r, h):
        low = 0 if r == 1 else rows - trimmed
        weights = gathered(r, h)
        queries = q_ref[low : low + trimmed, head_columns(h)]
        both = dot(queries, weights[:, : 2 * hidden], 1, 0)
        gates, ups = both[:, :hidden], both[:, hidden:]
        hid = (gates * jax.nn.sigmoid(gates) * ups).astype(BF16)
        return dot(hid, weights[:, 2 * hidden :], 1, 1).astype(BF16)

    def apply_first(h):
        out_ref[:trimmed, head_columns(h)] = apply(1, h)

    def apply_second(h):
        ag_wait(2, h)
        second = apply(2, h)
        low = rows - trimmed
        row = low + lax.broadcasted_iota(jnp.int32, (trimmed - low, 1), 0)
        out_ref[low:trimmed, head_columns(h)] = jnp.where(
            row < split_ref[0],
            out_ref[low:trimmed, head_columns(h)].astype(F32),
            second[: trimmed - low].astype(F32),
        ).astype(BF16)
        out_ref[trimmed:, head_columns(h)] = second[trimmed - low :]

    for load in loads:
        load.start()
    barrier = pltpu.get_barrier_semaphore()
    peers = [partner, y_peer, x_peer] + [device(zp, y0, c0) for zp in z_peers]
    for peer in peers:
        pl.semaphore_signal(barrier, inc=1, device_id=peer, device_id_type=MESH)
    for h in range(heads):
        for m in range(3):
            w[0, h, z0, y0, c0, :, m * hidden : (m + 1) * hidden] = initial(m, h).astype(BF16)
    pl.semaphore_wait(barrier, len(peers))
    for h in range(heads):
        ag_z(0, h)
    for load in loads:
        load.wait()

    stages = []
    for r in range(2):
        stages += [functools.partial(ag_y, r), functools.partial(ag_c, r)]
        if r == 0:
            stages.append(ag_x)
        stages += [functools.partial(stage, r) for stage in (gradient, rs_y, rs_z, update)]
    stages += [functools.partial(ag_y, 2), functools.partial(ag_c, 2), apply_second]
    order = [(s, stages[s]) for s in range(len(stages))] + [(10, apply_first)]

    def tick(t, carry):
        for s, stage in order:
            h = t - s

            @pl.when(jnp.logical_and(h >= 0, h < heads))
            def _():
                stage(h)

        return carry

    lax.fori_loop(0, len(stages) + heads - 1, tick, 0)

    def drain(h, carry):
        for y, zs in ((y0, z_peers), (y1, [z0] + z_peers)):
            for z in zs:
                ag_x_copy(h, z, y).wait_send()
        for r in range(3):
            along_y = [ag_y_copy(r, h, z) for z in range(nz)]
            for copy in ag_z_copies(r, h) + along_y + [ag_c_copy(r, h, y) for y in range(NY)]:
                copy.wait_send()
        for r in range(2):
            along_y = [rs_y_copy(r, h, z) for z in range(nz)]
            for copy in rs_z_copies(r, h) + along_y + [rs_c_copy(r, h, y) for y in range(NY)]:
                copy.wait_send()
        return carry

    lax.fori_loop(0, heads, drain, 0)


def fused_step(queries, keys, values, rates, split_row, fast_init):
    rows, features = queries.shape
    heads = rates.shape[1]
    width = features // heads
    hidden = fast_init.shape[1] // (3 * heads)
    owned = fast_init.shape[0]
    nz = lax.axis_size("tok") // (NY * NC)
    chunk = (owned, 3 * hidden)
    hbm = pl.BlockSpec(memory_space=pl.ANY)
    vmem = pl.BlockSpec(memory_space=pltpu.VMEM)
    dma = pltpu.SemaphoreType.DMA
    return pl.pallas_call(
        functools.partial(step_kernel, (heads, rows, width, hidden, nz, owned)),
        out_shape=jax.ShapeDtypeStruct((rows, features), BF16),
        in_specs=[hbm, hbm, hbm, vmem, pl.BlockSpec(memory_space=pltpu.SMEM), vmem],
        out_specs=vmem,
        scratch_shapes=[
            pltpu.VMEM((rows, features), BF16),
            pltpu.VMEM((rows, features), BF16),
            pltpu.VMEM((rows, features), BF16),
            pltpu.VMEM((3, heads, nz, NY, NC) + chunk, BF16),
            pltpu.VMEM((heads, nz, NY, NC) + chunk, F32),
            pltpu.VMEM((2, heads, nz, NY, NC) + chunk, BF16),
            pltpu.VMEM((2, heads, nz) + chunk, BF16),
            pltpu.VMEM((2, heads, nz, NY) + chunk, BF16),
            pltpu.VMEM((2, heads, nz) + chunk, BF16),
            pltpu.VMEM((2, heads, nz) + chunk, BF16),
            pltpu.VMEM((2, heads, nz) + chunk, BF16),
            pltpu.VMEM((heads,) + chunk, F32),
            pltpu.VMEM((heads,) + chunk, F32),
            dma((3,)),
            dma((3, heads, nz - 1)),
            dma((3, heads, nz)),
            dma((3, heads, nz)),
            dma((3, heads, nz)),
            dma((3, heads, NY)),
            dma((3, heads, NY)),
            dma((heads, nz, NY)),
            dma((heads, nz, NY)),
            dma((2, heads, NY)),
            dma((2, heads, NY)),
            dma((2, heads, nz)),
            dma((2, heads, nz)),
            dma((2, heads, nz - 1)),
            dma((2, heads, nz)),
        ],
        compiler_params=pltpu.CompilerParams(
            collective_id=0, has_side_effects=True, vmem_limit_bytes=60 * 1024 * 1024
        ),
        name="fast_weight_step",
    )(queries, keys, values, rates.T, split_row, fast_init)


def gather_weights(shard, heads, hidden):
    gathered = lax.all_gather(shard, "tok", axis=0, tiled=True)
    return gathered.reshape(gathered.shape[0], 3, heads, hidden)


def products(stacked, gathered):
    gates = jnp.einsum("rhj,jhf->rhf", stacked, gathered[:, 0], preferred_element_type=jnp.float32)
    ups = jnp.einsum("rhj,jhf->rhf", stacked, gathered[:, 1], preferred_element_type=jnp.float32)
    return (gates, ups)


def segment_gradient(key_heads, value_heads, rates, keep, gates, ups, down, owned_rows):
    sigma = jax.nn.sigmoid(gates)
    active = gates * sigma
    hidden_act = (active * ups).astype(jnp.bfloat16)
    scale = -(rates * keep[:, None].astype(jnp.float32))
    outer_grad = (scale[:, :, None] * value_heads.astype(jnp.float32)).astype(jnp.bfloat16)
    hidden_grad = jnp.einsum("rhj,jhf->rhf", outer_grad, down, preferred_element_type=jnp.float32)
    backward_gate_grad = (hidden_grad * ups * sigma * (1.0 + gates * (1.0 - sigma))).astype(
        jnp.bfloat16
    )
    backward_up_grad = (hidden_grad * active).astype(jnp.bfloat16)
    grad_gate = jnp.einsum(
        "rhj,rhf->jhf", key_heads, backward_gate_grad, preferred_element_type=jnp.float32
    )
    grad_up = jnp.einsum(
        "rhj,rhf->jhf", key_heads, backward_up_grad, preferred_element_type=jnp.float32
    )
    grad_gate, grad_up = (grad_gate, grad_up)
    grad_down = jnp.einsum(
        "rhj,rhf->jhf", outer_grad, hidden_act, preferred_element_type=jnp.float32
    )
    return lax.psum_scatter(
        jnp.stack([grad_gate, grad_up, grad_down], axis=1).reshape(
            lax.axis_size("tok") * owned_rows, -1
        ),
        "tok",
        scatter_dimension=0,
        tiled=True,
    )


def owner_update(state, momentum, gradient, initial, heads, hidden):
    momentum = MOMENTUM_DECAY * momentum + gradient
    moved = (state - momentum).reshape(state.shape[0], 3 * heads, hidden)
    base = initial.reshape(state.shape[0], 3 * heads, hidden)
    target = jnp.sqrt(jnp.mean(base * base, axis=-1, keepdims=True))
    current = jnp.sqrt(jnp.mean(moved * moved, axis=-1, keepdims=True) + EPSILON)
    return ((moved * (target / current)).reshape(state.shape), momentum)


def apply_fast(gates, ups, down):
    query_hidden = (jax.nn.silu(gates) * ups).astype(jnp.bfloat16)
    return jnp.einsum("rhf,jhf->rhj", query_hidden, down, preferred_element_type=jnp.float32)


def per_device(queries, keys, values, rates, split_row, fast_init):
    token_rows = queries.shape[0]
    heads = rates.shape[1]
    width = queries.shape[1] // heads
    hidden = fast_init.shape[1] // (3 * heads)
    owned_rows = fast_init.shape[0]
    query_heads = queries.reshape(token_rows, heads, width)
    key_heads = keys.reshape(token_rows, heads, width)
    value_heads = values.reshape(token_rows, heads, width)
    first = jnp.arange(token_rows) < split_row[0]
    second = jnp.logical_not(first)
    momentum = jnp.zeros_like(fast_init)
    gathered = gather_weights(fast_init.astype(jnp.bfloat16), heads, hidden)
    gates, ups = products(key_heads, gathered)
    gradient = segment_gradient(
        key_heads, value_heads, rates, first, gates, ups, gathered[:, 2], owned_rows
    )
    state, momentum = owner_update(fast_init, momentum, gradient, fast_init, heads, hidden)
    gathered = gather_weights(state.astype(jnp.bfloat16), heads, hidden)
    down = gathered[:, 2]
    stacked = jnp.concatenate([query_heads, key_heads], axis=0)
    gates, ups = products(stacked, gathered)
    out_first = apply_fast(gates[:token_rows], ups[:token_rows], down)
    gradient = segment_gradient(
        key_heads,
        value_heads,
        rates,
        second,
        gates[token_rows:],
        ups[token_rows:],
        down,
        owned_rows,
    )
    state, momentum = owner_update(state, momentum, gradient, fast_init, heads, hidden)
    gathered = gather_weights(state.astype(jnp.bfloat16), heads, hidden)
    gates, ups = products(query_heads, gathered)
    out_second = apply_fast(gates, ups, gathered[:, 2])
    mixed = jnp.where(first[:, None, None], out_first, out_second)
    return mixed.astype(jnp.bfloat16).reshape(token_rows, heads * width)


def plan(*args):
    size = lax.axis_size("tok")
    small = size // (NY * NC) in (2, 3, 4) and size % (NY * NC) == 0
    if small and lax.axis_size("groups") == 2 and args[5].shape[0] % 16 == 0:
        return fused_step(*args)
    return per_device(*args)


def solution(mesh):
    in_specs = (
        P(("groups", "tok"), None),
        P(("groups", "tok"), None),
        P(("groups", "tok"), None),
        P(("groups", "tok"), None),
        P(("groups", "tok")),
        P("tok", None),
    )
    out_specs = P(("groups", "tok"), None)
    return jax.shard_map(
        plan, mesh=mesh, in_specs=in_specs, out_specs=out_specs, check_vma=False
    )
```

```python
import functools

import jax
import jax.numpy as jnp
from jax import lax
from jax.experimental import pallas as pl
from jax.experimental.pallas import tpu as pltpu
from jax.sharding import PartitionSpec as P

MOMENTUM_DECAY = 0.9
EPSILON = 1e-06
MESH = pl.DeviceIdType.MESH
BF16 = jnp.bfloat16
F32 = jnp.float32
NY, NC = 2, 2


def dot(lhs, rhs, lhs_dim, rhs_dim):
    return lax.dot_general(
        lhs, rhs, (((lhs_dim,), (rhs_dim,)), ((), ())), preferred_element_type=F32
    )


def step_kernel(
    dims,
    q_hbm, k_hbm, v_hbm, rates_ref, split_ref, init_ref, out_hbm,
    out_ref, q_ref, k_ref, v_ref, w, own, grad, half, core_in, quarter, y_in, z_in, state, momentum,
    load_sem, store_sem, agz_s, agz_r, agy_s, agy_r, agc_s, agc_r, agx_s, agx_r,
    rsc_s, rsc_r, rsy_s, rsy_r, rsz_s, rsz_r,
):
    heads, rows, width, hidden, nz, owned = dims
    me = lax.axis_index("tok")
    g0 = lax.axis_index("groups")
    c0 = lax.rem(me, NC)
    y0 = lax.rem(me // NC, NY)
    z0 = me // (NC * NY)
    c1, y1 = 1 - c0, 1 - y0
    z_steps = [2, 1] + list(range(3, nz)) if nz > 3 else list(range(1, nz))
    z_peers = [lax.rem(z0 + i, nz) for i in z_steps]
    trimmed = rows - rows // 4

    def device(z, y, c):
        return {"tok": (z * NY + y) * NC + c}

    x_peer = {"groups": 1 - g0}
    gathered_here = pl.ds(pl.multiple_of(g0 * hidden, hidden), 2 * hidden)
    sent_across = pl.ds(pl.multiple_of(g0 * 2 * hidden, hidden), hidden)
    got_across = pl.ds(pl.multiple_of((1 - g0) * 2 * hidden, hidden), hidden)

    partner, y_peer = device(z0, y0, c1), device(z0, y1, c0)

    def remote(src, dst, send_sem, recv_sem, target):
        return pltpu.make_async_remote_copy(
            src_ref=src, dst_ref=dst, send_sem=send_sem, recv_sem=recv_sem,
            device_id=target, device_id_type=MESH,
        )

    loads = [
        pltpu.make_async_copy(src, dst, load_sem.at[i])
        for i, (src, dst) in enumerate(((k_hbm, k_ref), (v_hbm, v_ref), (q_hbm, q_ref)))
    ]

    def shard(r, h, z, y):
        if r == 0:
            return w.at[r, h, z, y, c0, :, gathered_here]
        return w.at[r, h, z, y, c0]

    def ag_x_copy(h, z, y):
        part = w.at[0, h, z, y, c0, :, sent_across]
        return remote(part, part, agx_s.at[h, z, y], agx_r.at[h, z, y], x_peer)

    def ag_z_copies(r, h):
        mine = shard(r, h, z0, y0)
        return [
            remote(mine, mine, agz_s.at[r, h, i], agz_r.at[r, h, z0], device(zp, y0, c0))
            for i, zp in enumerate(z_peers)
        ]

    def ag_y_copy(r, h, z):
        mine = shard(r, h, z, y0)
        return remote(mine, mine, agy_s.at[r, h, z], agy_r.at[r, h, z], y_peer)

    def ag_c_copy(r, h, y):
        mine = w.at[r, h, :, y, c0]
        return remote(mine, mine, agc_s.at[r, h, y], agc_r.at[r, h, y], partner)

    def rs_c_copy(r, h, y):
        return remote(
            grad.at[r, h, :, y, c1], core_in.at[r, h, :, y],
            rsc_s.at[r, h, y], rsc_r.at[r, h, y], partner,
        )

    def rs_y_copy(r, h, z):
        return remote(
            half.at[r, h, z], y_in.at[r, h, z], rsy_s.at[r, h, z], rsy_r.at[r, h, z], y_peer
        )

    def rs_z_copies(r, h):
        return [
            remote(
                quarter.at[r, h, zp], z_in.at[r, h, z0], rsz_s.at[r, h, i], rsz_r.at[r, h, z0],
                device(zp, y0, c0),
            )
            for i, zp in enumerate(z_peers)
        ]

    def ag_z(r, h):
        for copy in ag_z_copies(r, h):
            copy.start()
        ag_y_copy(r, h, z0).start()

    def ag_y(r, h):
        for i, zp in reversed(list(enumerate(z_peers))):
            there = shard(r, h, zp, y0)
            remote(there, there, agz_s.at[r, h, i], agz_r.at[r, h, zp], y_peer).wait_recv()
            ag_y_copy(r, h, zp).start()
            if r == 0:
                ag_x_copy(h, zp, y0).start()
        if r > 0:
            ag_c_copy(r, h, y0).start()

    def ag_c(r, h):
        for z in [z0] + z_peers[::-1]:
            there = shard(r, h, z, y1)
            remote(there, there, agy_s.at[r, h, z], agy_r.at[r, h, z], y_peer).wait_recv()
            if r == 0:
                ag_x_copy(h, z, y1).start()
        if r > 0:
            ag_c_copy(r, h, y1).start()

    def ag_x(h):
        for y, zs in ((y0, z_peers[::-1]), (y1, [z0] + z_peers[::-1])):
            for z in zs:
                there = w.at[0, h, z, y, c0, :, got_across]
                remote(there, there, agx_s.at[h, z, y], agx_r.at[h, z, y], x_peer).wait_recv()
            ag_c_copy(0, h, y).start()

    def ag_wait(r, h):
        for y in range(NY):
            there = w.at[r, h, :, y, c1]
            remote(there, there, agc_s.at[r, h, y], agc_r.at[r, h, y], partner).wait_recv()

    def gathered(r, h):
        return w[r, h].reshape(width, 3 * hidden)

    def head_columns(h):
        return pl.ds(pl.multiple_of(h * width, width), width)

    def gradient(r, h):
        ag_wait(r, h)
        low = 0 if r == 0 else rows - trimmed
        weights = gathered(r, h)
        keys = k_ref[low : low + trimmed, head_columns(h)]
        values = v_ref[low : low + trimmed, head_columns(h)]
        row = low + lax.broadcasted_iota(jnp.int32, (trimmed, 1), 0)
        first = row < split_ref[0]
        keep = first if r == 0 else jnp.logical_not(first)
        across = lax.broadcasted_iota(jnp.int32, (trimmed, trimmed), 0)
        along = lax.broadcasted_iota(jnp.int32, (trimmed, trimmed), 1)
        rate_row = rates_ref[pl.ds(h, 1), low : low + trimmed]
        rate = jnp.sum(jnp.where(across == along, rate_row, 0.0), axis=1, keepdims=True)
        scale = -(rate * keep.astype(F32))
        dout = (scale * values.astype(F32)).astype(BF16)
        both = dot(keys, weights[:, : 2 * hidden], 1, 0)
        dhid = dot(dout, weights[:, 2 * hidden :], 1, 0)
        gates, ups = both[:, :hidden], both[:, hidden:]
        sigma = jax.nn.sigmoid(gates)
        active = gates * sigma
        hid = (active * ups).astype(BF16)
        dg = (dhid * ups * sigma * (1.0 + gates * (1.0 - sigma))).astype(BF16)
        du = (dhid * active).astype(BF16)
        to_both = dot(keys, jnp.concatenate([dg, du], axis=1), 0, 0)
        to_down = dot(dout, hid, 0, 0)
        to_both = to_both.reshape(nz, NY, NC, owned, 2 * hidden)
        to_down = to_down.reshape(nz, NY, NC, owned, hidden)
        grad[r, h, :, :, :, :, : 2 * hidden] = to_both.astype(BF16)
        grad[r, h, :, :, :, :, 2 * hidden :] = to_down.astype(BF16)
        rs_c_copy(r, h, y1).start()
        rs_c_copy(r, h, y0).start()
        own[h, :, :, :, :, : 2 * hidden] = to_both
        own[h, :, :, :, :, 2 * hidden :] = to_down

    def rs_y(r, h):
        rs_c_copy(r, h, y1).wait_recv()
        for z in z_peers + [z0]:
            half[r, h, z] = (own[h, z, y1, c0] + core_in[r, h, z, y1].astype(F32)).astype(BF16)
            rs_y_copy(r, h, z).start()

    def pair_sum(r, h, z):
        rs_y_copy(r, h, z).wait_recv()
        return own[h, z, y0, c0] + core_in[r, h, z, y0].astype(F32) + y_in[r, h, z].astype(F32)

    def rs_z(r, h):
        rs_c_copy(r, h, y0).wait_recv()
        for zp, copy in zip(z_peers, rs_z_copies(r, h)):
            quarter[r, h, zp] = pair_sum(r, h, zp).astype(BF16)
            copy.start()

    def initial(m, h):
        return init_ref[:, pl.ds(pl.multiple_of((m * heads + h) * hidden, hidden), hidden)]

    def update(r, h):
        total = pair_sum(r, h, z0)
        for i, zp in enumerate(z_peers):
            there = z_in.at[r, h, zp]
            remote(there, there, rsz_s.at[r, h, i], rsz_r.at[r, h, zp], y_peer).wait_recv()
            total = total + z_in[r, h, zp].astype(F32)
        for m in range(3):
            part = slice(m * hidden, (m + 1) * hidden)
            base = initial(m, h)
            if r == 0:
                moment = total[:, part]
                moved = base - moment
                momentum[h, :, part] = moment
            else:
                moved = state[h, :, part] - (MOMENTUM_DECAY * momentum[h, :, part] + total[:, part])
            target = jnp.sqrt(jnp.mean(base * base, axis=-1, keepdims=True))
            current = jnp.sqrt(jnp.mean(moved * moved, axis=-1, keepdims=True) + EPSILON)
            new = moved * (target / current)
            if r == 0:
                state[h, :, part] = new
            w[r + 1, h, z0, y0, c0, :, part] = new.astype(BF16)
        ag_z(r + 1, h)

    def apply(r, h):
        low = 0 if r == 1 else rows - trimmed
        weights = gathered(r, h)
        queries = q_ref[low : low + trimmed, head_columns(h)]
        both = dot(queries, weights[:, : 2 * hidden], 1, 0)
        gates, ups = both[:, :hidden], both[:, hidden:]
        hid = (gates * jax.nn.sigmoid(gates) * ups).astype(BF16)
        return dot(hid, weights[:, 2 * hidden :], 1, 1).astype(BF16)

    def store(h):
        columns = head_columns(h)
        return pltpu.make_async_copy(
            out_ref.at[:, columns], out_hbm.at[:, columns], store_sem.at[h]
        )

    def apply_first(h):
        out_ref[:trimmed, head_columns(h)] = apply(1, h)

    def apply_second(h):
        ag_wait(2, h)
        second = apply(2, h)
        low = rows - trimmed
        row = low + lax.broadcasted_iota(jnp.int32, (trimmed - low, 1), 0)
        out_ref[low:trimmed, head_columns(h)] = jnp.where(
            row < split_ref[0],
            out_ref[low:trimmed, head_columns(h)].astype(F32),
            second[: trimmed - low].astype(F32),
        ).astype(BF16)
        out_ref[trimmed:, head_columns(h)] = second[trimmed - low :]
        store(h).start()

    for load in loads:
        load.start()
    barrier = pltpu.get_barrier_semaphore()
    peers = [partner, y_peer, x_peer] + [device(zp, y0, c0) for zp in z_peers]
    for peer in peers:
        pl.semaphore_signal(barrier, inc=1, device_id=peer, device_id_type=MESH)
    for h in range(heads):
        for m in range(3):
            w[0, h, z0, y0, c0, :, m * hidden : (m + 1) * hidden] = initial(m, h).astype(BF16)
    pl.semaphore_wait(barrier, len(peers))
    for h in range(heads):
        ag_z(0, h)
    for load in loads:
        load.wait()

    stages = []
    for r in range(2):
        stages += [functools.partial(ag_y, r), functools.partial(ag_c, r)]
        if r == 0:
            stages.append(ag_x)
        stages += [functools.partial(stage, r) for stage in (gradient, rs_y, rs_z, update)]
    stages += [functools.partial(ag_y, 2), functools.partial(ag_c, 2), apply_second]
    order = [(s, stages[s]) for s in range(len(stages))] + [(10, apply_first)]

    def tick(t, carry):
        for s, stage in order:
            h = t - s

            @pl.when(jnp.logical_and(h >= 0, h < heads))
            def _():
                stage(h)

        return carry

    lax.fori_loop(0, len(stages) + heads - 1, tick, 0)

    def drain(h, carry):
        store(h).wait()
        for y, zs in ((y0, z_peers), (y1, [z0] + z_peers)):
            for z in zs:
                ag_x_copy(h, z, y).wait_send()
        for r in range(3):
            along_y = [ag_y_copy(r, h, z) for z in range(nz)]
            for copy in ag_z_copies(r, h) + along_y + [ag_c_copy(r, h, y) for y in range(NY)]:
                copy.wait_send()
        for r in range(2):
            along_y = [rs_y_copy(r, h, z) for z in range(nz)]
            for copy in rs_z_copies(r, h) + along_y + [rs_c_copy(r, h, y) for y in range(NY)]:
                copy.wait_send()
        return carry

    lax.fori_loop(0, heads, drain, 0)


def fused_step(queries, keys, values, rates, split_row, fast_init):
    rows, features = queries.shape
    heads = rates.shape[1]
    width = features // heads
    hidden = fast_init.shape[1] // (3 * heads)
    owned = fast_init.shape[0]
    nz = lax.axis_size("tok") // (NY * NC)
    chunk = (owned, 3 * hidden)
    hbm = pl.BlockSpec(memory_space=pl.ANY)
    vmem = pl.BlockSpec(memory_space=pltpu.VMEM)
    dma = pltpu.SemaphoreType.DMA
    return pl.pallas_call(
        functools.partial(step_kernel, (heads, rows, width, hidden, nz, owned)),
        out_shape=jax.ShapeDtypeStruct((rows, features), BF16),
        in_specs=[hbm, hbm, hbm, vmem, pl.BlockSpec(memory_space=pltpu.SMEM), vmem],
        out_specs=hbm,
        scratch_shapes=[
            pltpu.VMEM((rows, features), BF16),
            pltpu.VMEM((rows, features), BF16),
            pltpu.VMEM((rows, features), BF16),
            pltpu.VMEM((rows, features), BF16),
            pltpu.VMEM((3, heads, nz, NY, NC) + chunk, BF16),
            pltpu.VMEM((heads, nz, NY, NC) + chunk, F32),
            pltpu.VMEM((2, heads, nz, NY, NC) + chunk, BF16),
            pltpu.VMEM((2, heads, nz) + chunk, BF16),
            pltpu.VMEM((2, heads, nz, NY) + chunk, BF16),
            pltpu.VMEM((2, heads, nz) + chunk, BF16),
            pltpu.VMEM((2, heads, nz) + chunk, BF16),
            pltpu.VMEM((2, heads, nz) + chunk, BF16),
            pltpu.VMEM((heads,) + chunk, F32),
            pltpu.VMEM((heads,) + chunk, F32),
            dma((3,)),
            dma((heads,)),
            dma((3, heads, nz - 1)),
            dma((3, heads, nz)),
            dma((3, heads, nz)),
            dma((3, heads, nz)),
            dma((3, heads, NY)),
            dma((3, heads, NY)),
            dma((heads, nz, NY)),
            dma((heads, nz, NY)),
            dma((2, heads, NY)),
            dma((2, heads, NY)),
            dma((2, heads, nz)),
            dma((2, heads, nz)),
            dma((2, heads, nz - 1)),
            dma((2, heads, nz)),
        ],
        compiler_params=pltpu.CompilerParams(
            collective_id=0, has_side_effects=True, vmem_limit_bytes=60 * 1024 * 1024
        ),
        name="fast_weight_step",
    )(queries, keys, values, rates.T, split_row, fast_init)


def gather_weights(shard, heads, hidden):
    gathered = lax.all_gather(shard, "tok", axis=0, tiled=True)
    return gathered.reshape(gathered.shape[0], 3, heads, hidden)


def products(stacked, gathered):
    gates = jnp.einsum("rhj,jhf->rhf", stacked, gathered[:, 0], preferred_element_type=jnp.float32)
    ups = jnp.einsum("rhj,jhf->rhf", stacked, gathered[:, 1], preferred_element_type=jnp.float32)
    return (gates, ups)


def segment_gradient(key_heads, value_heads, rates, keep, gates, ups, down, owned_rows):
    sigma = jax.nn.sigmoid(gates)
    active = gates * sigma
    hidden_act = (active * ups).astype(jnp.bfloat16)
    scale = -(rates * keep[:, None].astype(jnp.float32))
    outer_grad = (scale[:, :, None] * value_heads.astype(jnp.float32)).astype(jnp.bfloat16)
    hidden_grad = jnp.einsum("rhj,jhf->rhf", outer_grad, down, preferred_element_type=jnp.float32)
    backward_gate_grad = (hidden_grad * ups * sigma * (1.0 + gates * (1.0 - sigma))).astype(
        jnp.bfloat16
    )
    backward_up_grad = (hidden_grad * active).astype(jnp.bfloat16)
    grad_gate = jnp.einsum(
        "rhj,rhf->jhf", key_heads, backward_gate_grad, preferred_element_type=jnp.float32
    )
    grad_up = jnp.einsum(
        "rhj,rhf->jhf", key_heads, backward_up_grad, preferred_element_type=jnp.float32
    )
    grad_gate, grad_up = (grad_gate, grad_up)
    grad_down = jnp.einsum(
        "rhj,rhf->jhf", outer_grad, hidden_act, preferred_element_type=jnp.float32
    )
    return lax.psum_scatter(
        jnp.stack([grad_gate, grad_up, grad_down], axis=1).reshape(
            lax.axis_size("tok") * owned_rows, -1
        ),
        "tok",
        scatter_dimension=0,
        tiled=True,
    )


def owner_update(state, momentum, gradient, initial, heads, hidden):
    momentum = MOMENTUM_DECAY * momentum + gradient
    moved = (state - momentum).reshape(state.shape[0], 3 * heads, hidden)
    base = initial.reshape(state.shape[0], 3 * heads, hidden)
    target = jnp.sqrt(jnp.mean(base * base, axis=-1, keepdims=True))
    current = jnp.sqrt(jnp.mean(moved * moved, axis=-1, keepdims=True) + EPSILON)
    return ((moved * (target / current)).reshape(state.shape), momentum)


def apply_fast(gates, ups, down):
    query_hidden = (jax.nn.silu(gates) * ups).astype(jnp.bfloat16)
    return jnp.einsum("rhf,jhf->rhj", query_hidden, down, preferred_element_type=jnp.float32)


def per_device(queries, keys, values, rates, split_row, fast_init):
    token_rows = queries.shape[0]
    heads = rates.shape[1]
    width = queries.shape[1] // heads
    hidden = fast_init.shape[1] // (3 * heads)
    owned_rows = fast_init.shape[0]
    query_heads = queries.reshape(token_rows, heads, width)
    key_heads = keys.reshape(token_rows, heads, width)
    value_heads = values.reshape(token_rows, heads, width)
    first = jnp.arange(token_rows) < split_row[0]
    second = jnp.logical_not(first)
    momentum = jnp.zeros_like(fast_init)
    gathered = gather_weights(fast_init.astype(jnp.bfloat16), heads, hidden)
    gates, ups = products(key_heads, gathered)
    gradient = segment_gradient(
        key_heads, value_heads, rates, first, gates, ups, gathered[:, 2], owned_rows
    )
    state, momentum = owner_update(fast_init, momentum, gradient, fast_init, heads, hidden)
    gathered = gather_weights(state.astype(jnp.bfloat16), heads, hidden)
    down = gathered[:, 2]
    stacked = jnp.concatenate([query_heads, key_heads], axis=0)
    gates, ups = products(stacked, gathered)
    out_first = apply_fast(gates[:token_rows], ups[:token_rows], down)
    gradient = segment_gradient(
        key_heads,
        value_heads,
        rates,
        second,
        gates[token_rows:],
        ups[token_rows:],
        down,
        owned_rows,
    )
    state, momentum = owner_update(state, momentum, gradient, fast_init, heads, hidden)
    gathered = gather_weights(state.astype(jnp.bfloat16), heads, hidden)
    gates, ups = products(query_heads, gathered)
    out_second = apply_fast(gates, ups, gathered[:, 2])
    mixed = jnp.where(first[:, None, None], out_first, out_second)
    return mixed.astype(jnp.bfloat16).reshape(token_rows, heads * width)


def plan(*args):
    size = lax.axis_size("tok")
    small = size // (NY * NC) in (2, 3, 4) and size % (NY * NC) == 0
    if small and lax.axis_size("groups") == 2 and args[5].shape[0] % 16 == 0:
        return fused_step(*args)
    return per_device(*args)


def solution(mesh):
    in_specs = (
        P(("groups", "tok"), None),
        P(("groups", "tok"), None),
        P(("groups", "tok"), None),
        P(("groups", "tok"), None),
        P(("groups", "tok")),
        P("tok", None),
    )
    out_specs = P(("groups", "tok"), None)
    return jax.shard_map(
        plan, mesh=mesh, in_specs=in_specs, out_specs=out_specs, check_vma=False
    )
```

```python
import functools

import jax
import jax.numpy as jnp
from jax import lax
from jax.experimental import pallas as pl
from jax.experimental.pallas import tpu as pltpu
from jax.sharding import PartitionSpec as P

MOMENTUM_DECAY = 0.9
EPSILON = 1e-06
MESH = pl.DeviceIdType.MESH
BF16 = jnp.bfloat16
F32 = jnp.float32
NY, NC = 2, 2


def dot(lhs, rhs, lhs_dim, rhs_dim):
    return lax.dot_general(
        lhs, rhs, (((lhs_dim,), (rhs_dim,)), ((), ())), preferred_element_type=F32
    )


def step_kernel(
    dims,
    q_hbm, k_hbm, v_hbm, rates_ref, split_ref, init_ref, out_hbm,
    out_ref, q_ref, k_ref, v_ref, w, own, grad, half, core_in, quarter, y_in, z_in, state, momentum,
    load_sem, store_sem, agz_s, agz_r, agy_s, agy_r, agc_s, agc_r, agx_s, agx_r,
    rsc_s, rsc_r, rsy_s, rsy_r, rsz_s, rsz_r,
):
    heads, rows, width, hidden, nz, owned = dims
    me = lax.axis_index("tok")
    g0 = lax.axis_index("groups")
    c0 = lax.rem(me, NC)
    y0 = lax.rem(me // NC, NY)
    z0 = me // (NC * NY)
    c1, y1 = 1 - c0, 1 - y0
    z_steps = [2, 1] + list(range(3, nz)) if nz > 3 else list(range(1, nz))
    z_peers = [lax.rem(z0 + i, nz) for i in z_steps]
    trimmed = rows - rows // 4

    def device(z, y, c):
        return {"tok": (z * NY + y) * NC + c}

    x_peer = {"groups": 1 - g0}
    gathered_here = pl.ds(pl.multiple_of(g0 * hidden, hidden), 2 * hidden)
    sent_across = pl.ds(pl.multiple_of(g0 * 2 * hidden, hidden), hidden)
    got_across = pl.ds(pl.multiple_of((1 - g0) * 2 * hidden, hidden), hidden)

    partner, y_peer = device(z0, y0, c1), device(z0, y1, c0)

    def remote(src, dst, send_sem, recv_sem, target):
        return pltpu.make_async_remote_copy(
            src_ref=src, dst_ref=dst, send_sem=send_sem, recv_sem=recv_sem,
            device_id=target, device_id_type=MESH,
        )

    loads = [
        pltpu.make_async_copy(src, dst, load_sem.at[i])
        for i, (src, dst) in enumerate(((k_hbm, k_ref), (v_hbm, v_ref), (q_hbm, q_ref)))
    ]

    def shard(r, h, z, y):
        if r == 0:
            return w.at[r, h, z, y, c0, :, gathered_here]
        return w.at[r, h, z, y, c0]

    def ag_x_copy(h, z, y):
        part = w.at[0, h, z, y, c0, :, sent_across]
        return remote(part, part, agx_s.at[h, z, y], agx_r.at[h, z, y], x_peer)

    def ag_z_copies(r, h):
        mine = shard(r, h, z0, y0)
        return [
            remote(mine, mine, agz_s.at[r, h, i], agz_r.at[r, h, z0], device(zp, y0, c0))
            for i, zp in enumerate(z_peers)
        ]

    def ag_y_copy(r, h, z):
        mine = shard(r, h, z, y0)
        return remote(mine, mine, agy_s.at[r, h, z], agy_r.at[r, h, z], y_peer)

    def ag_c_copy(r, h, y):
        mine = w.at[r, h, :, y, c0]
        return remote(mine, mine, agc_s.at[r, h, y], agc_r.at[r, h, y], partner)

    def rs_c_copy(r, h, y):
        return remote(
            grad.at[r, h, :, y, c1], core_in.at[r, h, :, y],
            rsc_s.at[r, h, y], rsc_r.at[r, h, y], partner,
        )

    def rs_y_copy(r, h, z):
        return remote(
            half.at[r, h, z], y_in.at[r, h, z], rsy_s.at[r, h, z], rsy_r.at[r, h, z], y_peer
        )

    def rs_z_copies(r, h):
        return [
            remote(
                quarter.at[r, h, zp], z_in.at[r, h, z0], rsz_s.at[r, h, i], rsz_r.at[r, h, z0],
                device(zp, y0, c0),
            )
            for i, zp in enumerate(z_peers)
        ]

    def ag_z(r, h):
        for copy in ag_z_copies(r, h):
            copy.start()
        ag_y_copy(r, h, z0).start()

    def ag_y(r, h):
        for i, zp in reversed(list(enumerate(z_peers))):
            there = shard(r, h, zp, y0)
            remote(there, there, agz_s.at[r, h, i], agz_r.at[r, h, zp], y_peer).wait_recv()
            ag_y_copy(r, h, zp).start()
            if r == 0:
                ag_x_copy(h, zp, y0).start()
        if r > 0:
            ag_c_copy(r, h, y0).start()

    def ag_c(r, h):
        for z in [z0] + z_peers[::-1]:
            there = shard(r, h, z, y1)
            remote(there, there, agy_s.at[r, h, z], agy_r.at[r, h, z], y_peer).wait_recv()
            if r == 0:
                ag_x_copy(h, z, y1).start()
        if r > 0:
            ag_c_copy(r, h, y1).start()

    def ag_x(h):
        for y, zs in ((y0, z_peers[::-1]), (y1, [z0] + z_peers[::-1])):
            for z in zs:
                there = w.at[0, h, z, y, c0, :, got_across]
                remote(there, there, agx_s.at[h, z, y], agx_r.at[h, z, y], x_peer).wait_recv()
            ag_c_copy(0, h, y).start()

    def ag_wait(r, h):
        for y in range(NY):
            there = w.at[r, h, :, y, c1]
            remote(there, there, agc_s.at[r, h, y], agc_r.at[r, h, y], partner).wait_recv()

    def gathered(r, h):
        return w[r, h].reshape(width, 3 * hidden)

    def head_columns(h):
        return pl.ds(pl.multiple_of(h * width, width), width)

    def gradient(r, h):
        ag_wait(r, h)
        low = 0 if r == 0 else rows - trimmed
        weights = gathered(r, h)
        keys = k_ref[low : low + trimmed, head_columns(h)]
        values = v_ref[low : low + trimmed, head_columns(h)]
        row = low + lax.broadcasted_iota(jnp.int32, (trimmed, 1), 0)
        first = row < split_ref[0]
        keep = first if r == 0 else jnp.logical_not(first)
        across = lax.broadcasted_iota(jnp.int32, (trimmed, trimmed), 0)
        along = lax.broadcasted_iota(jnp.int32, (trimmed, trimmed), 1)
        rate_row = rates_ref[pl.ds(h, 1), low : low + trimmed]
        rate = jnp.sum(jnp.where(across == along, rate_row, 0.0), axis=1, keepdims=True)
        scale = -(rate * keep.astype(F32))
        dout = (scale * values.astype(F32)).astype(BF16)
        both = dot(keys, weights[:, : 2 * hidden], 1, 0)
        dhid = dot(dout, weights[:, 2 * hidden :], 1, 0)
        gates, ups = both[:, :hidden], both[:, hidden:]
        sigma = jax.nn.sigmoid(gates)
        active = gates * sigma
        hid = (active * ups).astype(BF16)
        dg = (dhid * ups * sigma * (1.0 + gates * (1.0 - sigma))).astype(BF16)
        du = (dhid * active).astype(BF16)
        to_both = dot(keys, jnp.concatenate([dg, du], axis=1), 0, 0)
        to_down = dot(dout, hid, 0, 0)
        to_both = to_both.reshape(nz, NY, NC, owned, 2 * hidden)
        to_down = to_down.reshape(nz, NY, NC, owned, hidden)
        grad[r, h, :, :, :, :, : 2 * hidden] = to_both.astype(BF16)
        grad[r, h, :, :, :, :, 2 * hidden :] = to_down.astype(BF16)
        rs_c_copy(r, h, y1).start()
        rs_c_copy(r, h, y0).start()
        own[h, :, :, :, :, : 2 * hidden] = to_both
        own[h, :, :, :, :, 2 * hidden :] = to_down

    def rs_y(r, h):
        rs_c_copy(r, h, y1).wait_recv()
        for z in z_peers + [z0]:
            half[r, h, z] = (own[h, z, y1, c0] + core_in[r, h, z, y1].astype(F32)).astype(BF16)
            rs_y_copy(r, h, z).start()

    def pair_sum(r, h, z):
        rs_y_copy(r, h, z).wait_recv()
        return own[h, z, y0, c0] + core_in[r, h, z, y0].astype(F32) + y_in[r, h, z].astype(F32)

    def rs_z(r, h):
        rs_c_copy(r, h, y0).wait_recv()
        for zp, copy in zip(z_peers, rs_z_copies(r, h)):
            quarter[r, h, zp] = pair_sum(r, h, zp).astype(BF16)
            copy.start()

    def initial(m, h):
        return init_ref[:, pl.ds(pl.multiple_of((m * heads + h) * hidden, hidden), hidden)]

    def update(r, h):
        total = pair_sum(r, h, z0)
        for i, zp in enumerate(z_peers):
            there = z_in.at[r, h, zp]
            remote(there, there, rsz_s.at[r, h, i], rsz_r.at[r, h, zp], y_peer).wait_recv()
            total = total + z_in[r, h, zp].astype(F32)
        for m in range(3):
            part = slice(m * hidden, (m + 1) * hidden)
            base = initial(m, h)
            if r == 0:
                moment = total[:, part]
                moved = base - moment
                momentum[h, :, part] = moment
            else:
                moved = state[h, :, part] - (MOMENTUM_DECAY * momentum[h, :, part] + total[:, part])
            target = jnp.sqrt(jnp.mean(base * base, axis=-1, keepdims=True))
            current = jnp.sqrt(jnp.mean(moved * moved, axis=-1, keepdims=True) + EPSILON)
            new = moved * (target / current)
            if r == 0:
                state[h, :, part] = new
            w[r + 1, h, z0, y0, c0, :, part] = new.astype(BF16)
        ag_z(r + 1, h)

    def apply(r, h):
        low = 0 if r == 1 else rows - trimmed
        weights = gathered(r, h)
        queries = q_ref[low : low + trimmed, head_columns(h)]
        both = dot(queries, weights[:, : 2 * hidden], 1, 0)
        gates, ups = both[:, :hidden], both[:, hidden:]
        hid = (gates * jax.nn.sigmoid(gates) * ups).astype(BF16)
        return dot(hid, weights[:, 2 * hidden :], 1, 1).astype(BF16)

    def store(h):
        columns = head_columns(h)
        return pltpu.make_async_copy(
            out_ref.at[:, columns], out_hbm.at[:, columns], store_sem.at[h]
        )

    def apply_first(h):
        out_ref[:trimmed, head_columns(h)] = apply(1, h)

    def apply_second(h):
        ag_wait(2, h)
        second = apply(2, h)
        low = rows - trimmed
        row = low + lax.broadcasted_iota(jnp.int32, (trimmed - low, 1), 0)
        out_ref[low:trimmed, head_columns(h)] = jnp.where(
            row < split_ref[0],
            out_ref[low:trimmed, head_columns(h)].astype(F32),
            second[: trimmed - low].astype(F32),
        ).astype(BF16)
        out_ref[trimmed:, head_columns(h)] = second[trimmed - low :]
        store(h).start()

    for load in loads:
        load.start()
    barrier = pltpu.get_barrier_semaphore()
    peers = [partner, y_peer, x_peer] + [device(zp, y0, c0) for zp in z_peers]
    for peer in peers:
        pl.semaphore_signal(barrier, inc=1, device_id=peer, device_id_type=MESH)
    for h in range(heads):
        for m in range(3):
            w[0, h, z0, y0, c0, :, m * hidden : (m + 1) * hidden] = initial(m, h).astype(BF16)
    pl.semaphore_wait(barrier, len(peers))
    for h in range(heads):
        ag_z(0, h)

    stages = []
    for r in range(2):
        stages += [functools.partial(ag_y, r), functools.partial(ag_c, r)]
        if r == 0:
            stages.append(ag_x)
        stages += [functools.partial(stage, r) for stage in (gradient, rs_y, rs_z, update)]
    stages += [functools.partial(ag_y, 2), functools.partial(ag_c, 2), apply_second]
    order = [(s, stages[s]) for s in range(len(stages))] + [(10, apply_first)]

    def tick(t, carry):
        @pl.when(t == 2)
        def _():
            for load in loads:
                load.wait()

        for s, stage in order:
            h = t - s

            @pl.when(jnp.logical_and(h >= 0, h < heads))
            def _():
                stage(h)

        return carry

    lax.fori_loop(0, len(stages) + heads - 1, tick, 0)

    def drain(h, carry):
        store(h).wait()
        for y, zs in ((y0, z_peers), (y1, [z0] + z_peers)):
            for z in zs:
                ag_x_copy(h, z, y).wait_send()
        for r in range(3):
            along_y = [ag_y_copy(r, h, z) for z in range(nz)]
            for copy in ag_z_copies(r, h) + along_y + [ag_c_copy(r, h, y) for y in range(NY)]:
                copy.wait_send()
        for r in range(2):
            along_y = [rs_y_copy(r, h, z) for z in range(nz)]
            for copy in rs_z_copies(r, h) + along_y + [rs_c_copy(r, h, y) for y in range(NY)]:
                copy.wait_send()
        return carry

    lax.fori_loop(0, heads, drain, 0)


def fused_step(queries, keys, values, rates, split_row, fast_init):
    rows, features = queries.shape
    heads = rates.shape[1]
    width = features // heads
    hidden = fast_init.shape[1] // (3 * heads)
    owned = fast_init.shape[0]
    nz = lax.axis_size("tok") // (NY * NC)
    chunk = (owned, 3 * hidden)
    hbm = pl.BlockSpec(memory_space=pl.ANY)
    vmem = pl.BlockSpec(memory_space=pltpu.VMEM)
    dma = pltpu.SemaphoreType.DMA
    return pl.pallas_call(
        functools.partial(step_kernel, (heads, rows, width, hidden, nz, owned)),
        out_shape=jax.ShapeDtypeStruct((rows, features), BF16),
        in_specs=[hbm, hbm, hbm, vmem, pl.BlockSpec(memory_space=pltpu.SMEM), vmem],
        out_specs=hbm,
        scratch_shapes=[
            pltpu.VMEM((rows, features), BF16),
            pltpu.VMEM((rows, features), BF16),
            pltpu.VMEM((rows, features), BF16),
            pltpu.VMEM((rows, features), BF16),
            pltpu.VMEM((3, heads, nz, NY, NC) + chunk, BF16),
            pltpu.VMEM((heads, nz, NY, NC) + chunk, F32),
            pltpu.VMEM((2, heads, nz, NY, NC) + chunk, BF16),
            pltpu.VMEM((2, heads, nz) + chunk, BF16),
            pltpu.VMEM((2, heads, nz, NY) + chunk, BF16),
            pltpu.VMEM((2, heads, nz) + chunk, BF16),
            pltpu.VMEM((2, heads, nz) + chunk, BF16),
            pltpu.VMEM((2, heads, nz) + chunk, BF16),
            pltpu.VMEM((heads,) + chunk, F32),
            pltpu.VMEM((heads,) + chunk, F32),
            dma((3,)),
            dma((heads,)),
            dma((3, heads, nz - 1)),
            dma((3, heads, nz)),
            dma((3, heads, nz)),
            dma((3, heads, nz)),
            dma((3, heads, NY)),
            dma((3, heads, NY)),
            dma((heads, nz, NY)),
            dma((heads, nz, NY)),
            dma((2, heads, NY)),
            dma((2, heads, NY)),
            dma((2, heads, nz)),
            dma((2, heads, nz)),
            dma((2, heads, nz - 1)),
            dma((2, heads, nz)),
        ],
        compiler_params=pltpu.CompilerParams(
            collective_id=0, has_side_effects=True, vmem_limit_bytes=60 * 1024 * 1024
        ),
        name="fast_weight_step",
    )(queries, keys, values, rates.T, split_row, fast_init)


def gather_weights(shard, heads, hidden):
    gathered = lax.all_gather(shard, "tok", axis=0, tiled=True)
    return gathered.reshape(gathered.shape[0], 3, heads, hidden)


def products(stacked, gathered):
    gates = jnp.einsum("rhj,jhf->rhf", stacked, gathered[:, 0], preferred_element_type=jnp.float32)
    ups = jnp.einsum("rhj,jhf->rhf", stacked, gathered[:, 1], preferred_element_type=jnp.float32)
    return (gates, ups)


def segment_gradient(key_heads, value_heads, rates, keep, gates, ups, down, owned_rows):
    sigma = jax.nn.sigmoid(gates)
    active = gates * sigma
    hidden_act = (active * ups).astype(jnp.bfloat16)
    scale = -(rates * keep[:, None].astype(jnp.float32))
    outer_grad = (scale[:, :, None] * value_heads.astype(jnp.float32)).astype(jnp.bfloat16)
    hidden_grad = jnp.einsum("rhj,jhf->rhf", outer_grad, down, preferred_element_type=jnp.float32)
    backward_gate_grad = (hidden_grad * ups * sigma * (1.0 + gates * (1.0 - sigma))).astype(
        jnp.bfloat16
    )
    backward_up_grad = (hidden_grad * active).astype(jnp.bfloat16)
    grad_gate = jnp.einsum(
        "rhj,rhf->jhf", key_heads, backward_gate_grad, preferred_element_type=jnp.float32
    )
    grad_up = jnp.einsum(
        "rhj,rhf->jhf", key_heads, backward_up_grad, preferred_element_type=jnp.float32
    )
    grad_gate, grad_up = (grad_gate, grad_up)
    grad_down = jnp.einsum(
        "rhj,rhf->jhf", outer_grad, hidden_act, preferred_element_type=jnp.float32
    )
    return lax.psum_scatter(
        jnp.stack([grad_gate, grad_up, grad_down], axis=1).reshape(
            lax.axis_size("tok") * owned_rows, -1
        ),
        "tok",
        scatter_dimension=0,
        tiled=True,
    )


def owner_update(state, momentum, gradient, initial, heads, hidden):
    momentum = MOMENTUM_DECAY * momentum + gradient
    moved = (state - momentum).reshape(state.shape[0], 3 * heads, hidden)
    base = initial.reshape(state.shape[0], 3 * heads, hidden)
    target = jnp.sqrt(jnp.mean(base * base, axis=-1, keepdims=True))
    current = jnp.sqrt(jnp.mean(moved * moved, axis=-1, keepdims=True) + EPSILON)
    return ((moved * (target / current)).reshape(state.shape), momentum)


def apply_fast(gates, ups, down):
    query_hidden = (jax.nn.silu(gates) * ups).astype(jnp.bfloat16)
    return jnp.einsum("rhf,jhf->rhj", query_hidden, down, preferred_element_type=jnp.float32)


def per_device(queries, keys, values, rates, split_row, fast_init):
    token_rows = queries.shape[0]
    heads = rates.shape[1]
    width = queries.shape[1] // heads
    hidden = fast_init.shape[1] // (3 * heads)
    owned_rows = fast_init.shape[0]
    query_heads = queries.reshape(token_rows, heads, width)
    key_heads = keys.reshape(token_rows, heads, width)
    value_heads = values.reshape(token_rows, heads, width)
    first = jnp.arange(token_rows) < split_row[0]
    second = jnp.logical_not(first)
    momentum = jnp.zeros_like(fast_init)
    gathered = gather_weights(fast_init.astype(jnp.bfloat16), heads, hidden)
    gates, ups = products(key_heads, gathered)
    gradient = segment_gradient(
        key_heads, value_heads, rates, first, gates, ups, gathered[:, 2], owned_rows
    )
    state, momentum = owner_update(fast_init, momentum, gradient, fast_init, heads, hidden)
    gathered = gather_weights(state.astype(jnp.bfloat16), heads, hidden)
    down = gathered[:, 2]
    stacked = jnp.concatenate([query_heads, key_heads], axis=0)
    gates, ups = products(stacked, gathered)
    out_first = apply_fast(gates[:token_rows], ups[:token_rows], down)
    gradient = segment_gradient(
        key_heads,
        value_heads,
        rates,
        second,
        gates[token_rows:],
        ups[token_rows:],
        down,
        owned_rows,
    )
    state, momentum = owner_update(state, momentum, gradient, fast_init, heads, hidden)
    gathered = gather_weights(state.astype(jnp.bfloat16), heads, hidden)
    gates, ups = products(query_heads, gathered)
    out_second = apply_fast(gates, ups, gathered[:, 2])
    mixed = jnp.where(first[:, None, None], out_first, out_second)
    return mixed.astype(jnp.bfloat16).reshape(token_rows, heads * width)


def plan(*args):
    size = lax.axis_size("tok")
    small = size // (NY * NC) in (2, 3, 4) and size % (NY * NC) == 0
    if small and lax.axis_size("groups") == 2 and args[5].shape[0] % 16 == 0:
        return fused_step(*args)
    return per_device(*args)


def solution(mesh):
    in_specs = (
        P(("groups", "tok"), None),
        P(("groups", "tok"), None),
        P(("groups", "tok"), None),
        P(("groups", "tok"), None),
        P(("groups", "tok")),
        P("tok", None),
    )
    out_specs = P(("groups", "tok"), None)
    return jax.shard_map(
        plan, mesh=mesh, in_specs=in_specs, out_specs=out_specs, check_vma=False
    )
```
